256 devices in a mesh: row: 64 (over y, x_hi, z), col: 4 (over x_lo, core).
Axes of the slice: x: 4 (x_hi: 2, x_lo: 2; x = x_hi * 2 + x_lo), y: 4, z: 8, core: 2. Of those that a mesh axis runs over, the one named last changes fastest.
Arguments:
- operator: bfloat16 [32768, 32768], P('row', 'col'), may hold values from -0.0068359375 to 0.0068359375
- rhs: float32 [32, 32768], P(None, 'row'), may hold values from -72 to 72
- bodies: int32 [32768], P('row'), may hold values from 0 to 63, as said below
- weights: float32 [32768], P('row'), may hold values from 0.5 to 1.5
Outputs:
- basis: float32 [128, 32768], P(None, ('row', 'col'))
- hess: float32 [128, 96], replicated
- start_factor: float32 [32, 32], replicated
The draws below stay inside these ranges and needn't reach their ends.
Inputs may be any that keep to these rules, and one draw needn't show every extreme that they name: Every one of the 64 bodies has at least one node.
All inputs are finite; a program needn't handle non-finite values.
Results may differ from the reference program's by a relative error of at most 0.0025.
Values may be sent and summed in bfloat16 or wider, within the bound.
A program may use at most 64 MiB of HBM per device.

```python
import jax
import jax.numpy as jnp
from jax import lax

N = 32768
S = 32
BODIES = 64
STEPS = 3


def body_index_of(key):
    position = jnp.arange(N, dtype=jnp.int32)
    random_ids = jax.random.randint(jax.random.fold_in(key, 11), (N,), 0, BODIES, dtype=jnp.int32)
    ordered = jnp.where(position < BODIES, position, random_ids)
    return jax.random.permutation(jax.random.fold_in(key, 12), ordered).astype(jnp.int32)


def draw_bodies(key, part):
    return body_index_of(key)


def draw_rhs(key, part):
    body_index = body_index_of(key)
    position = jnp.arange(N, dtype=jnp.float32)
    rigid_motion = jnp.clip(jax.random.normal(jax.random.fold_in(key, 21), (S, BODIES), jnp.float32), -4.0, 4.0)
    noise_part = jnp.clip(jax.random.normal(jax.random.fold_in(key, 22), (S, N), jnp.float32), -4.0, 4.0)
    amplitude = 1.0 + 3.0 * position / N
    values = amplitude[None, :] * (rigid_motion[:, body_index] + noise_part)
    return values.astype(jnp.float32)


def shard_levels(stream_key, dims, cuts, smallest, largest):
    factor_of = 1.0
    for axis_at, shards_of in cuts:
        steps = jax.random.uniform(jax.random.fold_in(jax.random.fold_in(stream_key, 6), axis_at), (shards_of,), jnp.float32, smallest / len(cuts), largest / len(cuts))
        factor_of = factor_of * jnp.repeat(jnp.exp(steps), dims[axis_at] // shards_of).reshape((-1,) + (1,) * (len(dims) - 1 - axis_at))
    return factor_of


def noise(rng, dims, spread, reach, cuts=(), kind=jnp.bfloat16):
    level = shard_levels(rng, dims, cuts, -0.22, 0.18) if cuts else 1.0
    array = jax.random.normal(rng, dims, jnp.float32) * spread * level
    return jnp.minimum(jnp.maximum(array, -reach), reach).astype(kind)


def setup_inputs(seed: int = 0) -> dict:
    key_of = jax.random.split(jax.random.key(seed), 5)
    operator = noise(key_of[0], (N, N), (25 * N) ** -0.5, 0.0068359375, ((0, 64), (1, 4)))
    rhs = draw_rhs(jax.random.fold_in(key_of[4], 71), 0)
    bodies = draw_bodies(jax.random.fold_in(key_of[4], 71), 0)
    weights = jnp.clip(1.0 + 0.1 * jax.random.normal(key_of[3], (N,), jnp.float32), 0.5, 1.5)
    return {"operator": operator, "rhs": rhs, "bodies": bodies, "weights": weights}


def product_t(left, right):
    return lax.dot_general(left.astype(jnp.float32), right.astype(jnp.float32), (((1,), (1,)), ((), ())), precision=lax.Precision.HIGHEST, preferred_element_type=jnp.float32)

def image_of(current, operator, onehot, weights):
    current_low = current.astype(jnp.bfloat16)
    block_rows = min(N, 2048)
    op_blocks = operator.reshape(N // block_rows, block_rows, N)

    def apply_rows(op_rows):
        return lax.dot_general(current_low.astype(jnp.float32), op_rows.astype(jnp.float32), (((1,), (1,)), ((), ())), preferred_element_type=jnp.float32)
    coupled = lax.map(apply_rows, op_blocks)
    coupled = jnp.transpose(coupled, (1, 0, 2)).reshape(current.shape[0], N)
    scaled = current_low.astype(jnp.float32) * weights[None, :]
    body_means = jnp.dot(scaled, onehot, precision=lax.Precision.HIGHEST) * (BODIES / N)
    completion = weights[None, :] * product_t(body_means, onehot)
    return 0.5 * current + coupled + completion

def reference(operator, rhs, bodies, weights):
    onehot = (bodies[:, None] == jnp.arange(BODIES, dtype=jnp.int32)[None, :]).astype(jnp.float32)
    gram_start = product_t(rhs, rhs) / N
    start_low = jnp.linalg.cholesky(gram_start)
    basis_list = [lax.linalg.triangular_solve(start_low, rhs, left_side=True, lower=True)]
    columns = []
    for step_index in range(STEPS):
        stacked = jnp.concatenate(basis_list, axis=0)
        image_block = image_of(basis_list[-1], operator, onehot, weights)
        first_coef = product_t(stacked, image_block) / N
        residual_one = image_block - jnp.dot(first_coef.T, stacked, precision=lax.Precision.HIGHEST)
        gram_block = product_t(residual_one, residual_one) / N
        factor_low = jnp.linalg.cholesky(gram_block)
        basis_list.append(lax.linalg.triangular_solve(factor_low, residual_one, left_side=True, lower=True))
        pieces = [first_coef, factor_low.T]
        below = (STEPS - 1 - step_index) * S
        if below > 0:
            pieces.append(jnp.zeros((below, S), jnp.float32))
        columns.append(jnp.concatenate(pieces, axis=0))
    return (jnp.concatenate(basis_list, axis=0), jnp.concatenate(columns, axis=1), start_low)
```

```python
import jax
import jax.numpy as jnp
from jax import lax
from jax.experimental import pallas as pl
from jax.experimental.pallas import tpu as pltpu
from jax.sharding import Mesh
from jax.sharding import PartitionSpec as P

N = 32768
S = 32
BODIES = 64
STEPS = 3
ROWS = 512
COLS = 8192
Q = 128
AXES = ("y", "xh", "z", "xl", "co")
ROW = ("y", "xh", "z")
COL = ("xl", "co")
MESH = pl.DeviceIdType.MESH
F32 = jnp.float32
BF16 = jnp.bfloat16
OP_CHUNKS = 4
MM_CHUNK = 2048


def mm(a, b):
    return lax.dot_general(
        a, b, (((1,), (0,)), ((), ())), precision=lax.Precision.HIGHEST, preferred_element_type=F32
    )


def mm_t(a, b):
    return lax.dot_general(
        a, b, (((1,), (1,)), ((), ())), precision=lax.Precision.HIGHEST, preferred_element_type=F32
    )


def factor(gram):
    row_id = lax.broadcasted_iota(jnp.int32, (S, Q), 0)
    lane_id = lax.broadcasted_iota(jnp.int32, (S, Q), 1)
    eye = (lane_id == row_id + S).astype(F32)
    work = jnp.concatenate([gram, jnp.zeros((S, Q - S), F32)], axis=1) + eye
    for k in range(S):
        pivot = work[k : k + 1, k : k + 1]
        r = lax.rsqrt(pivot)
        r = r * (1.5 - 0.5 * pivot * r * r)
        row = work[k : k + 1, :] * r
        col = work[:, k : k + 1] * r
        update = jnp.where(row_id > k, work - col * row, work)
        work = jnp.where(row_id == k, row, update)
    upper = jnp.where(lane_id >= row_id, work, 0.0)[:, :S]
    return upper, work[:, S : 2 * S]


def kernel(
    op_hbm,
    rhs_ref,
    bodies_ref,
    weights_ref,
    basis_ref,
    hess_ref,
    start_ref,
    op,
    stack,
    images,
    means,
    low,
    gathered,
    part,
    parts_in,
    pay0,
    pay1,
    half_in,
    z_buf,
    x_buf,
    y_buf,
    total,
    op_sem,
    g_send,
    g_recv,
    r_send,
    r_recv,
    a_send,
    a_recv,
):
    y, xh, z, xl, co = (lax.axis_index(a) for a in AXES)
    c = xl * 2 + co
    x = xh * 2 + xl
    mine = ((xh * 8 + z) * 4 + c) * Q
    holds = jnp.logical_and(xl == y // 2, co == y % 2)

    loads = []
    width = COLS // OP_CHUNKS
    for i in range(OP_CHUNKS):
        window = pl.ds(i * width, width)
        loads.append(pltpu.make_async_copy(op_hbm.at[:, window], op.at[:, window], op_sem.at[i]))
        loads[-1].start()

    def gather_to(i):
        return ((y + i % 4) % 4, (xh + (i // 4) % 2) % 2, (z + i // 8) % 8, y // 2, y % 2)

    def gather_from(i):
        return (c, i // 32, (i // 4) % 8, (i // 2) % 2, i % 2)

    def z_peer(i):
        return (y, xh, (z + i) % 8, xl, co)

    def x_peer(i):
        t = (x + i) % 4
        return (y, t // 2, z, t % 2, co)

    def y_peer(i):
        return ((y + i) % 4, xh, z, xl, co)

    def col_peer(i):
        t = (c + i) % 4
        return (y, xh, z, t // 2, t % 2)

    other_core = (y, xh, z, xl, 1 - co)

    barrier = pltpu.get_barrier_semaphore()

    def greet(count, peer, first):
        def body(i, carry):
            pl.semaphore_signal(barrier, inc=1, device_id=peer(i), device_id_type=MESH)
            return carry

        lax.fori_loop(first, count, body, 0)
        return count - first

    greeted = greet(64, gather_to, 0)
    greeted += greet(64, gather_from, 0)
    greeted += greet(8, z_peer, 1)
    greeted += greet(4, x_peer, 1)
    greeted += greet(4, y_peer, 1)
    greeted += greet(4, col_peer, 1)

    quarter = pl.ds(pl.multiple_of(c * Q, Q), Q)
    weight = weights_ref[:, quarter]
    body = bodies_ref[:, quarter]
    ids = lax.broadcasted_iota(jnp.int32, (BODIES, Q), 0)
    stack[pl.ds(0, BODIES), :] = jnp.where(ids == body, weight, 0.0)
    stack[pl.ds(BODIES, 4 * S), :] = jnp.zeros((4 * S, Q), F32)
    means[...] = jnp.zeros_like(means)
    hess_ref[...] = jnp.zeros_like(hess_ref)
    images[...] = jnp.zeros_like(images)
    newest = rhs_ref[:, quarter]

    pl.semaphore_wait(barrier, greeted)

    pending = []

    def remote(src, dst, send, recv, device):
        return pltpu.make_async_remote_copy(
            src_ref=src, dst_ref=dst, send_sem=send, recv_sem=recv, device_id=device, device_id_type=MESH
        )

    def await_bytes(ref, sem):
        pltpu.make_async_copy(ref, ref, sem).wait()

    def reduced(j, pay):
        rows = pay.shape[0]
        h = rows // 2
        mine_rows = pl.ds(pl.multiple_of(co * h, h), h)
        theirs = pl.ds(pl.multiple_of((1 - co) * h, h), h)
        part_in = half_in.at[j, pl.ds(0, h), :]
        remote(pay.at[theirs, :], part_in, a_send.at[j, 0], a_recv.at[j, 0], other_core).start()
        pending.append((pay.at[theirs, :], a_send.at[j, 0], 1))
        await_bytes(part_in, a_recv.at[j, 0])
        value = pay[mine_rows, :] + half_in[j, :h, :]
        for stage, (buf, here, count, peer) in enumerate(
            ((z_buf, z, 8, z_peer), (x_buf, x, 4, x_peer), (y_buf, y, 4, y_peer))
        ):
            slot = buf.at[j, here, pl.ds(0, h), :]
            buf[j, here, pl.ds(0, h), :] = value
            for i in range(1, count):
                remote(slot, slot, a_send.at[j, 1 + stage], a_recv.at[j, 1 + stage], peer(i)).start()
            pending.append((buf.at[j, pl.ds(0, count - 1), pl.ds(0, h), :], a_send.at[j, 1 + stage], 1))
            await_bytes(buf.at[j, pl.ds(0, count - 1), pl.ds(0, h), :], a_recv.at[j, 1 + stage])
            value = buf[j, 0, :h, :]
            for i in range(1, count):
                value = value + buf[j, i, :h, :]
        total[j, mine_rows, :] = value
        out = total.at[j, mine_rows, :]
        remote(out, out, a_send.at[j, 4], a_recv.at[j, 4], other_core).start()
        pending.append((out, a_send.at[j, 4], 1))
        await_bytes(total.at[j, theirs, :], a_recv.at[j, 4])

    pred = None
    for j in range(STEPS + 1):
        last = j == STEPS
        stack[pl.ds(BODIES + S * j, S), :] = newest
        if not last:
            low[j] = newest.astype(BF16)
            slot = gathered.at[j, :, pl.ds(pl.multiple_of(mine, Q), Q)]

            def send(i, carry):
                own = jnp.logical_and(i == 0, holds)

                @pl.when(jnp.logical_not(own))
                def _():
                    remote(low.at[j], slot, g_send.at[j], g_recv.at[j], gather_to(i)).start()

                @pl.when(own)
                def _():
                    pltpu.make_async_copy(low.at[j], slot, g_recv.at[j]).start()

                return carry

            lax.fori_loop(0, 64, send, 0)
        if last:
            pay0[j] = mm_t(newest, stack[pl.ds(BODIES, 4 * S), :])
            pay = pay0.at[j]
        elif j == 2:
            pay1[pl.ds(0, S), :] = mm_t(newest, stack[pl.ds(0, Q), :])
            pay1[pl.ds(S, S), :] = jnp.concatenate(
                [mm_t(newest, newest), jnp.zeros((S, Q - S), F32)], axis=1
            )
            pay = pay1
        else:
            pay0[j] = mm_t(newest, stack[pl.ds(0, Q), :])
            pay = pay0.at[j]
        reduced(j, pay)
        sums = total[j, :S, :] * (1.0 / N)
        if last:
            coef, gram = sums[:, : 3 * S], sums[:, 3 * S :]
        elif j == 2:
            coef, gram = sums[:, BODIES:], total[j, S : 2 * S, :S] * (1.0 / N)
        elif j == 1:
            coef, gram = sums[:, BODIES : BODIES + S], sums[:, BODIES + S :]
        else:
            coef, gram = None, sums[:, BODIES : BODIES + S]
        if coef is not None:
            gram = gram - mm_t(coef, coef)
        upper, inverse = factor(gram)
        if j == 0:
            start_ref[...] = upper.T
        else:
            full = coef + pred
            full = jnp.concatenate([full, jnp.zeros((S, Q - S * j), F32)], axis=1)
            hess_ref[pl.ds(0, S * j), pl.ds(S * (j - 1), S)] = full.T[: S * j, :]
            hess_ref[pl.ds(S * j, S), pl.ds(S * (j - 1), S)] = upper
        before = pl.ds(BODIES, S * j)
        upto = pl.ds(BODIES, S * (j + 1))
        residual = newest
        if j > 0:
            residual = residual - mm(coef, stack[before, :])
        vector = mm(inverse, residual)
        stack[pl.ds(BODIES + S * j, S), :] = vector
        basis_ref[pl.ds(S * j, S), :] = vector
        if last:
            break
        mean = sums[:, :BODIES] * BODIES
        raw = 0.5 * newest + mm(mean, stack[pl.ds(0, BODIES), :])
        mean = jnp.concatenate([mean, jnp.zeros((S, Q - BODIES), F32)], axis=1)
        if j > 0:
            mean = mean - mm(coef, means[pl.ds(0, S * j), :])
            raw = raw - mm(coef, images[pl.ds(0, S * j), :])
        mean = mm(inverse, mean)
        means[pl.ds(S * j, S), :] = mean
        lane = lax.broadcasted_iota(jnp.int32, (S, S * (j + 1)), 1)
        sub = lax.broadcasted_iota(jnp.int32, (S, S * (j + 1)), 0)
        pred = mm_t(mean, means[pl.ds(0, S * (j + 1)), :]) * (1.0 / BODIES)
        pred = pred + jnp.where(lane == sub + S * j, 0.5, 0.0)
        raw = mm(inverse, raw)
        shifted = mm(pred, stack[upto, :])

        if j == 0:
            for load in loads:
                load.wait()
        await_bytes(gathered.at[j], g_recv.at[j])
        acc = jnp.zeros((S, ROWS), F32)
        for i in range(COLS // MM_CHUNK):
            acc = acc + lax.dot_general(
                gathered[j, :, i * MM_CHUNK : (i + 1) * MM_CHUNK],
                op[:, i * MM_CHUNK : (i + 1) * MM_CHUNK],
                (((1,), (1,)), ((), ())),
                preferred_element_type=F32,
            )
        for i in range(4):
            part[j, i] = acc[:, i * Q : (i + 1) * Q]
        parts_in[j, c] = part[j, c]
        for i in range(1, 4):
            remote(part.at[j, (c + i) % 4], parts_in.at[j, c], r_send.at[j], r_recv.at[j], col_peer(i)).start()
        pending.append((part.at[j, pl.ds(0, 3)], r_send.at[j], 1))
        await_bytes(parts_in.at[j, pl.ds(0, 3)], r_recv.at[j])
        coupled = parts_in[j, 0] + parts_in[j, 1] + parts_in[j, 2] + parts_in[j, 3]
        image = mm(inverse, coupled) + raw
        images[pl.ds(S * j, S), :] = image
        newest = image - shifted

    for j in range(STEPS):

        def sent(i, carry):
            @pl.when(jnp.logical_not(jnp.logical_and(i == 0, holds)))
            def _():
                await_bytes(low.at[j], g_send.at[j])

            return carry

        lax.fori_loop(0, 64, sent, 0)
    for ref, sem, _ in pending:
        await_bytes(ref, sem)


def local(operator, rhs, bodies, weights):
    vmem = pl.BlockSpec(memory_space=pltpu.VMEM)
    dma = pltpu.SemaphoreType.DMA
    return pl.pallas_call(
        kernel,
        name="arnoldi",
        out_shape=(
            jax.ShapeDtypeStruct((4 * S, Q), F32),
            jax.ShapeDtypeStruct((4 * S, 3 * S), F32),
            jax.ShapeDtypeStruct((S, S), F32),
        ),
        in_specs=[pl.BlockSpec(memory_space=pl.ANY), vmem, vmem, vmem],
        out_specs=(vmem, vmem, vmem),
        scratch_shapes=[
            pltpu.VMEM((ROWS, COLS), BF16),
            pltpu.VMEM((BODIES + 4 * S, Q), F32),
            pltpu.VMEM((3 * S, Q), F32),
            pltpu.VMEM((3 * S, Q), F32),
            pltpu.VMEM((3, S, Q), BF16),
            pltpu.VMEM((3, S, COLS), BF16),
            pltpu.VMEM((3, 4, S, Q), F32),
            pltpu.VMEM((3, 4, S, Q), F32),
            pltpu.VMEM((4, S, Q), F32),
            pltpu.VMEM((2 * S, Q), F32),
            pltpu.VMEM((4, S, Q), F32),
            pltpu.VMEM((4, 8, S, Q), F32),
            pltpu.VMEM((4, 4, S, Q), F32),
            pltpu.VMEM((4, 4, S, Q), F32),
            pltpu.VMEM((4, 2 * S, Q), F32),
            dma((OP_CHUNKS,)),
            dma((3,)),
            dma((3,)),
            dma((3,)),
            dma((3,)),
            dma((4, 5)),
            dma((4, 5)),
        ],
        compiler_params=pltpu.CompilerParams(
            collective_id=0, has_side_effects=True, vmem_limit_bytes=40 * 2**20
        ),
    )(operator, rhs, bodies.reshape(1, ROWS), weights.reshape(1, ROWS))


def solution(mesh):
    split = Mesh(mesh.devices.reshape(4, 2, 8, 2, 2), AXES)
    placed = (P(ROW, COL), P(None, ROW), P(ROW), P(ROW))
    return jax.shard_map(
        local, mesh=split, in_specs=placed, out_specs=(P(None, ROW + COL), P(), P()), check_vma=False
    )
```

```python
import jax
import jax.numpy as jnp
from jax import lax
from jax.experimental import pallas as pl
from jax.experimental.pallas import tpu as pltpu
from jax.sharding import Mesh
from jax.sharding import PartitionSpec as P

N = 32768
S = 32
BODIES = 64
STEPS = 3
ROWS = 512
COLS = 8192
Q = 128
H = 16
AXES = ("y", "xh", "z", "xl", "co")
ROW = ("y", "xh", "z")
COL = ("xl", "co")
MESH = pl.DeviceIdType.MESH
F32 = jnp.float32
BF16 = jnp.bfloat16
OP_CHUNKS = 4
MM_CHUNK = 2048


def mm(a, b):
    return lax.dot_general(
        a, b, (((1,), (0,)), ((), ())), precision=lax.Precision.HIGHEST, preferred_element_type=F32
    )


def mm_t(a, b):
    return lax.dot_general(
        a, b, (((1,), (1,)), ((), ())), precision=lax.Precision.HIGHEST, preferred_element_type=F32
    )


def dot_low(a, b):
    return lax.dot_general(a, b, (((1,), (1,)), ((), ())), preferred_element_type=F32)


def factor(gram):
    row_id = lax.broadcasted_iota(jnp.int32, (S, Q), 0)
    lane_id = lax.broadcasted_iota(jnp.int32, (S, Q), 1)
    eye = (lane_id == row_id + S).astype(F32)
    work = jnp.concatenate([gram, jnp.zeros((S, Q - S), F32)], axis=1) + eye
    for k in range(S):
        pivot = work[k : k + 1, k : k + 1]
        r = lax.rsqrt(pivot)
        r = r * (1.5 - 0.5 * pivot * r * r)
        row = work[k : k + 1, :] * r
        col = work[:, k : k + 1] * r
        update = jnp.where(row_id > k, work - col * row, work)
        work = jnp.where(row_id == k, row, update)
    upper = jnp.where(lane_id >= row_id, work, 0.0)[:, :S]
    return upper, work[:, S : 2 * S]


def kernel(
    op_hbm,
    rhs_ref,
    bodies_ref,
    weights_ref,
    basis_ref,
    hess_ref,
    start_ref,
    op,
    ext,
    stack,
    wide,
    low,
    mid,
    part,
    parts_in,
    side_out,
    sides_in,
    table_out,
    table_in,
    pay0,
    zc_buf,
    xy_buf,
    total,
    op_sem,
    g_send,
    g0_recv,
    g1_recv,
    gm_recv,
    r_send,
    r_recv,
    s_send,
    s_recv,
    t_sem,
    a_send,
    a_recv,
):
    y, xh, z, xl, co = (lax.axis_index(a) for a in AXES)
    c = xl * 2 + co
    x = xh * 2 + xl
    mine = pl.ds(pl.multiple_of(((xh * 8 + z) * 4 + c) * Q, Q), Q)
    straight = xl == y // 2
    own1 = co == y % 2
    own0 = jnp.logical_and(jnp.logical_and(straight, own1), z % 2 == 0)

    loads = []
    width = COLS // OP_CHUNKS
    for i in range(OP_CHUNKS):
        window = pl.ds(i * width, width)
        loads.append(pltpu.make_async_copy(op_hbm.at[:, window], op.at[:, window], op_sem.at[i]))
        loads[-1].start()

    def plane_to(i):
        return ((y + i % 4) % 4, (xh + (i // 4) % 2) % 2, (z + i // 8) % 8, y // 2, y % 2)

    def plane_from(i):
        return (c, i // 32, (i // 4) % 8, (i // 2) % 2, i % 2)

    def a0_to(i):
        return ((y + 2 * (z % 2)) % 4, (xh + i % 2) % 2, (z + i // 2) % 8, y // 2, y % 2)

    def a0_from(i):
        return (c, i // 16, ((i // 4) % 4) * 2 + ((y + 4 - c) % 4) // 2, (i // 2) % 2, i % 2)

    def a1_to(i):
        return ((y + i % 4) % 4, xh, (z + i // 4) % 8, xl, y % 2)

    def a1_from(i):
        return (co + 2 * (i // 16), xh, (i // 2) % 8, xl, i % 2)

    def zc_peer(i):
        return (y, xh, (z + i // 2) % 8, xl, (co + i) % 2)

    def xy_peer(i):
        t = (x + i) % 4
        return ((y + i // 4) % 4, t // 2, z, t % 2, co)

    def col_peer(i):
        t = (c + i) % 4
        return (y, xh, z, t // 2, t % 2)

    near = z // 4 * 4
    order = ((xh, near), (1 - xh, near), (xh, 4 - near), (1 - xh, 4 - near))
    other_core = (y, xh, z, xl, 1 - co)

    barrier = pltpu.get_barrier_semaphore()

    def greet(count, peer, first):
        def body(i, carry):
            pl.semaphore_signal(barrier, inc=1, device_id=peer(i), device_id_type=MESH)
            return carry

        lax.fori_loop(first, count, body, 0)
        return count - first

    root = (y + 4 - c) % 2 == 0

    @pl.when(root)
    def _():
        greet(32, a0_from, 0)

    greeted = 16 + greet(32, a1_from, 0)
    greeted += greet(64, plane_from, 0)
    greeted += greet(16, zc_peer, 1)
    greeted += greet(16, xy_peer, 1)
    greeted += greet(4, col_peer, 1)

    quarter = pl.ds(pl.multiple_of(c * Q, Q), Q)
    weight = weights_ref[:, quarter]
    body = bodies_ref[:, quarter]
    ids = lax.broadcasted_iota(jnp.int32, (BODIES, Q), 0)
    stack[pl.ds(0, BODIES), :] = jnp.where(ids == body, weight, 0.0)
    stack[pl.ds(BODIES, 4 * S), :] = jnp.zeros((4 * S, Q), F32)
    wide[...] = jnp.zeros_like(wide)
    hess_ref[...] = jnp.zeros_like(hess_ref)
    newest = rhs_ref[:, quarter]
    table_out[pl.ds(0, 1), :] = weight
    table_out[pl.ds(1, 1), :] = body.astype(F32)

    pl.semaphore_wait(barrier, greeted)

    pending = []

    def remote(src, dst, send, recv, device):
        return pltpu.make_async_remote_copy(
            src_ref=src, dst_ref=dst, send_sem=send, recv_sem=recv, device_id=device, device_id_type=MESH
        )

    def await_bytes(ref, sem):
        pltpu.make_async_copy(ref, ref, sem).wait()

    def halves(pay):
        h = pay.shape[0] // 2
        return h, pl.ds(pl.multiple_of(co * h, h), h), pl.ds(pl.multiple_of((1 - co) * h, h), h)

    def sum_start(j, pay):
        h, own, theirs = halves(pay)
        here = z * 2 + co
        zc_buf[j, here, pl.ds(0, h), :] = pay[own, :]
        dst = zc_buf.at[j, here, pl.ds(0, h), :]
        for i in (8, 9, 7, 6, 10, 11, 5, 4, 12, 13, 3, 2, 14, 15, 1):
            src = pay.at[theirs if i % 2 else own, :]
            remote(src, dst, a_send.at[j, 0], a_recv.at[j, 0], zc_peer(i)).start()
        pending.append((zc_buf.at[j, pl.ds(0, 15), pl.ds(0, h), :], a_send.at[j, 0]))

    def summed(buf, j, h, count):
        terms = [buf[j, i, :h, :] for i in range(count)]
        while len(terms) > 1:
            terms = [terms[i] + terms[i + 1] for i in range(0, len(terms), 2)]
        return terms[0]

    def sum_middle(j, pay):
        h, _, _ = halves(pay)
        await_bytes(zc_buf.at[j, pl.ds(0, 15), pl.ds(0, h), :], a_recv.at[j, 0])
        here = y * 4 + x
        xy_buf[j, here, pl.ds(0, h), :] = summed(zc_buf, j, h, 16)
        slot = xy_buf.at[j, here, pl.ds(0, h), :]
        for i in (10, 9, 11, 14, 6, 8, 2, 13, 15, 5, 7, 1, 3, 4, 12):
            remote(slot, slot, a_send.at[j, 1], a_recv.at[j, 1], xy_peer(i)).start()
        pending.append((xy_buf.at[j, pl.ds(0, 15), pl.ds(0, h), :], a_send.at[j, 1]))

    def sum_finish(j, pay):
        h, own, theirs = halves(pay)
        await_bytes(xy_buf.at[j, pl.ds(0, 15), pl.ds(0, h), :], a_recv.at[j, 1])
        total[j, own, :] = summed(xy_buf, j, h, 16)
        out = total.at[j, own, :]
        remote(out, out, a_send.at[j, 2], a_recv.at[j, 2], other_core).start()
        pending.append((out, a_send.at[j, 2]))
        await_bytes(total.at[j, theirs, :], a_recv.at[j, 2])

    def top(j):
        return pl.ds(BODIES + S * j, H)

    def low_rows(j):
        return pl.ds(BODIES + S * j + H, H)

    def all_rows(j):
        return pl.ds(BODIES + S * j, S)


    def lanes0(xh_s, z_s):
        return pl.ds(pl.multiple_of((xh_s * 8 + z_s) * 4 * Q, 4 * Q), 4 * Q)

    def lanes1(x_s, z_s):
        return pl.ds(pl.multiple_of((((x_s // 2) * 8 + z_s) * 2 + x_s % 2) * 2 * Q, 2 * Q), 2 * Q)

    def root_for(z_s):
        return (y + 4 - c) % 4 == 2 * (z_s % 2)

    def loop(first, end, do):
        def body(i, carry):
            do(i)
            return carry

        lax.fori_loop(first, end, body, 0)

    def either(test, yes, no):
        pl.when(test)(yes)
        pl.when(jnp.logical_not(test))(no)

    def gather_start(j):
        src1, src0 = low.at[j, pl.ds(H, H), :], low.at[j, pl.ds(0, H), :]
        at1 = ext.at[low_rows(j), mine]
        at_mid = mid.at[j, z, :, pl.ds(pl.multiple_of(co * Q, Q), Q)]
        at0 = ext.at[top(j), mine]
        sem1, sem_mid, sem0 = g1_recv.at[j, x * 8 + z], gm_recv.at[j, z], g0_recv.at[j, xh * 8 + z]

        def spread1(dst, sem):
            loop(4, 32, lambda i: remote(src1, dst, g_send.at[j, 1], sem, a1_to(i)).start())
            loop(1, 4, lambda i: remote(src1, dst, g_send.at[j, 1], sem, a1_to(i)).start())
            either(
                own1,
                lambda: pltpu.make_async_copy(src1, dst, sem).start(),
                lambda: remote(src1, dst, g_send.at[j, 1], sem, a1_to(0)).start(),
            )

        either(straight, lambda: spread1(at1, sem1), lambda: spread1(at_mid, sem_mid))
        loop(1, 16, lambda i: remote(src0, at0, g_send.at[j, 0], sem0, a0_to(i)).start())
        either(
            own0,
            lambda: pltpu.make_async_copy(src0, at0, sem0).start(),
            lambda: remote(src0, at0, g_send.at[j, 0], sem0, a0_to(0)).start(),
        )

    def relay(j, d):
        z_s = (z + d) % 8
        here = ext.at[low_rows(j), lanes1(x, z_s)]
        sem1 = g1_recv.at[j, x * 8 + z_s]
        await_bytes(here, sem1)
        remote(here, here, g_send.at[j, 2], sem1, (y, 1 - xh, z, xl, co)).start()
        held = mid.at[j, z_s]
        await_bytes(held, gm_recv.at[j, z_s])
        for t in range(2):
            remote(held, here, g_send.at[j, 2], sem1, (y, t, z, 1 - xl, co)).start()

        @pl.when(root_for(z_s))
        def _():
            for xh_s in range(2):
                block = ext.at[top(j), lanes0(xh_s, z_s)]
                sem0 = g0_recv.at[j, xh_s * 8 + z_s]
                await_bytes(block, sem0)
                for i in (2, 1, 3):
                    remote(block, block, g_send.at[j, 3], sem0, ((y + i) % 4, xh, z, xl, co)).start()

    def await_chunk(j, xh_s, z_first):
        def one(k):
            z_s = z_first + k

            @pl.when(jnp.logical_not(root_for(z_s)))
            def _():
                await_bytes(ext.at[top(j), lanes0(xh_s, z_s)], g0_recv.at[j, xh_s * 8 + z_s])

            for xl_s in range(2):
                x_s = xh_s * 2 + xl_s

                @pl.when(x_s != x)
                def _():
                    await_bytes(ext.at[low_rows(j), lanes1(x_s, z_s)], g1_recv.at[j, x_s * 8 + z_s])

        loop(0, 4, one)

    def gather_sent(j):
        either(
            own0,
            lambda: await_bytes(ext.at[top(j), pl.ds(0, 15 * Q)], g_send.at[j, 0]),
            lambda: await_bytes(ext.at[top(j), pl.ds(0, 16 * Q)], g_send.at[j, 0]),
        )
        either(
            own1,
            lambda: await_bytes(ext.at[top(j), pl.ds(0, 31 * Q)], g_send.at[j, 1]),
            lambda: await_bytes(ext.at[top(j), pl.ds(0, 32 * Q)], g_send.at[j, 1]),
        )
        await_bytes(ext.at[top(j), pl.ds(0, 48 * Q)], g_send.at[j, 2])

        @pl.when(root)
        def _():
            await_bytes(ext.at[all_rows(j), pl.ds(0, 48 * Q)], g_send.at[j, 3])

    here = xh * 32 + z * 4 + c
    tables = pl.ds(0, 2)

    def table_start():
        src, dst = table_out.at[tables, :], table_in.at[here, tables, :]
        loop(1, 64, lambda i: remote(src, dst, t_sem.at[0], t_sem.at[1], plane_to(i)).start())
        either(
            jnp.logical_and(straight, own1),
            lambda: pltpu.make_async_copy(src, dst, t_sem.at[1]).start(),
            lambda: remote(src, dst, t_sem.at[0], t_sem.at[1], plane_to(0)).start(),
        )

    def table_finish():
        await_bytes(table_in.at[:, tables, :], t_sem.at[1])

        def build(i):
            plane = jnp.where(ids.astype(F32) == table_in[i, 1:2, :], table_in[i, 0:1, :], 0.0)
            ext[pl.ds(0, BODIES), pl.ds(pl.multiple_of(i * Q, Q), Q)] = plane.astype(BF16)

        loop(0, 64, build)

    def padded(value):
        return jnp.concatenate([value, jnp.zeros((S, Q - value.shape[1]), F32)], axis=1)

    lane = lax.broadcasted_iota(jnp.int32, (S, Q), 1)
    sub = lax.broadcasted_iota(jnp.int32, (S, Q), 0)
    pred = None

    def write_hess(j, coef, upper):
        full = padded(coef + pred).T
        hess_ref[pl.ds(0, S * j), pl.ds(S * (j - 1), S)] = full[: S * j, :]
        hess_ref[pl.ds(S * j, S), pl.ds(S * (j - 1), S)] = upper

    for j in range(STEPS):
        low[j] = newest.astype(BF16)
        gather_start(j)
        if j == 0:
            table_start()
        elif j == 1:
            start_ref[...] = upper.T
        else:
            write_hess(j - 1, coef, upper)
        if j > 0:
            pred = next_pred
        for d in (0, 1, 7, 2, 6, 3, 5, 4):
            relay(j, d)
        if j == 0:
            table_finish()
            for load in loads:
                load.wait()
        acc, side = None, None
        for i in range(4):
            xh_s, z_first = order[i]
            window = pl.ds(pl.multiple_of((xh_s * 8 + z_first) * 4 * Q, MM_CHUNK), MM_CHUNK)
            await_chunk(j, xh_s, z_first)
            term = dot_low(ext[all_rows(j), window], op[:, window])
            acc = term if acc is None else acc + term
            term = dot_low(ext[all_rows(j), window], ext[pl.ds(0, BODIES + S * (j + 1)), window])
            side = term if side is None else side + term
        for i in range(4):
            part[j, i] = acc[:, i * Q : (i + 1) * Q]
        for i in range(1, 4):
            remote(part.at[j, (c + i) % 4], parts_in.at[j, c], r_send.at[j], r_recv.at[j], col_peer(i)).start()
        pending.append((part.at[j, pl.ds(0, 3)], r_send.at[j]))
        parts_in[j, c] = part[j, c]
        blocks = 2 if j == 2 else 1
        side_out[j, 0] = padded(side[:, :Q]) if j < 1 else side[:, :Q]
        if blocks == 2:
            side_out[j, 1] = padded(side[:, Q:])
        out = side_out.at[j, pl.ds(0, blocks)]
        for i in range(1, 4):
            remote(out, sides_in.at[j, c, pl.ds(0, blocks)], s_send.at[j], s_recv.at[j], col_peer(i)).start()
        pending.append((sides_in.at[j, pl.ds(0, 3), pl.ds(0, blocks)], s_send.at[j]))
        for k in range(blocks):
            sides_in[j, c, k] = side_out[j, k]
        await_bytes(sides_in.at[j, pl.ds(0, 3), pl.ds(0, blocks)], s_recv.at[j])
        sums = [
            (sides_in[j, 0, k] + sides_in[j, 1, k]) + (sides_in[j, 2, k] + sides_in[j, 3, k]) for k in range(blocks)
        ]
        mean = sums[0][:, :BODIES] * (BODIES / N)
        raw = sums[0][:, BODIES:] * (1.0 / N)
        if j == 2:
            raw = jnp.concatenate([raw, sums[1][:, :S] * (1.0 / N)], axis=1)
        gram = raw[:, S * j : S * (j + 1)]
        coef = None
        if j > 0:
            coef = mm_t(padded(raw[:, : S * j]), wide[pl.ds(0, S * j), pl.ds(3 * Q, Q)])
            gram = gram - mm_t(coef, coef)
        upper, inverse = factor(gram)
        completion = mm(mean, stack[pl.ds(0, BODIES), :])
        await_bytes(parts_in.at[j, pl.ds(0, 3)], r_recv.at[j])
        coupled = (parts_in[j, 0] + parts_in[j, 1]) + (parts_in[j, 2] + parts_in[j, 3])
        image = 0.5 * newest + completion + coupled
        full = jnp.concatenate([newest, image, padded(mean), jnp.where(lane == sub + S * j, 1.0, 0.0)], axis=1)
        if j > 0:
            full = full - mm(coef, wide[pl.ds(0, S * j), :])
        full = mm(inverse, full)
        wide[pl.ds(S * j, S), :] = full
        upto = pl.ds(0, S * (j + 1))
        next_pred = mm_t(full[:, 2 * Q : 3 * Q], wide[upto, pl.ds(2 * Q, Q)]) * (1.0 / BODIES)
        next_pred = next_pred + jnp.where(lane == sub + S * j, 0.5, 0.0)[:, : S * (j + 1)]
        newest = full[:, Q : 2 * Q] - mm(next_pred, wide[upto, pl.ds(0, Q)])

    for j in range(STEPS):
        basis_ref[pl.ds(S * j, S), :] = wide[pl.ds(S * j, S), pl.ds(0, Q)]
        stack[pl.ds(BODIES + S * j, S), :] = wide[pl.ds(S * j, S), pl.ds(0, Q)]
    stack[pl.ds(BODIES + S * STEPS, S), :] = newest
    pay0[...] = mm_t(newest, stack[pl.ds(BODIES, 4 * S), :])
    sum_start(0, pay0)
    write_hess(2, coef, upper)
    pred = next_pred
    for i in range(STEPS):
        gather_sent(i)
    either(
        jnp.logical_and(straight, own1),
        lambda: await_bytes(table_in.at[pl.ds(0, 63), tables, :], t_sem.at[0]),
        lambda: await_bytes(table_in.at[:, tables, :], t_sem.at[0]),
    )
    sum_middle(0, pay0)
    sum_finish(0, pay0)
    sums = total[0] * (1.0 / N)
    coef, gram = sums[:, : 3 * S], sums[:, 3 * S :]
    gram = gram - mm_t(coef, coef)
    residual = newest - mm(coef, stack[pl.ds(BODIES, 3 * S), :])
    upper, inverse = factor(gram)
    basis_ref[pl.ds(3 * S, S), :] = mm(inverse, residual)
    write_hess(3, coef, upper)

    for ref, sem in pending:
        await_bytes(ref, sem)


def local(operator, rhs, bodies, weights):
    vmem = pl.BlockSpec(memory_space=pltpu.VMEM)
    dma = pltpu.SemaphoreType.DMA
    return pl.pallas_call(
        kernel,
        name="arnoldi",
        out_shape=(
            jax.ShapeDtypeStruct((4 * S, Q), F32),
            jax.ShapeDtypeStruct((4 * S, 3 * S), F32),
            jax.ShapeDtypeStruct((S, S), F32),
        ),
        in_specs=[pl.BlockSpec(memory_space=pl.ANY), vmem, vmem, vmem],
        out_specs=(vmem, vmem, vmem),
        scratch_shapes=[
            pltpu.VMEM((ROWS, COLS), BF16),
            pltpu.VMEM((BODIES + 3 * S, COLS), BF16),
            pltpu.VMEM((BODIES + 4 * S, Q), F32),
            pltpu.VMEM((3 * S, 4 * Q), F32),
            pltpu.VMEM((3, S, Q), BF16),
            pltpu.VMEM((3, 8, H, 2 * Q), BF16),
            pltpu.VMEM((3, 4, S, Q), F32),
            pltpu.VMEM((3, 4, S, Q), F32),
            pltpu.VMEM((3, 2, S, Q), F32),
            pltpu.VMEM((3, 4, 2, S, Q), F32),
            pltpu.VMEM((8, Q), F32),
            pltpu.VMEM((64, 8, Q), F32),
            pltpu.VMEM((S, Q), F32),
            pltpu.VMEM((1, 16, H, Q), F32),
            pltpu.VMEM((1, 16, H, Q), F32),
            pltpu.VMEM((1, S, Q), F32),
            dma((OP_CHUNKS,)),
            dma((3, 4)),
            dma((3, 16)),
            dma((3, 32)),
            dma((3, 8)),
            dma((3,)),
            dma((3,)),
            dma((3,)),
            dma((3,)),
            dma((2,)),
            dma((1, 3)),
            dma((1, 3)),
        ],
        compiler_params=pltpu.CompilerParams(
            collective_id=0, has_side_effects=True, vmem_limit_bytes=40 * 2**20
        ),
    )(operator, rhs, bodies.reshape(1, ROWS), weights.reshape(1, ROWS))


def solution(mesh):
    split = Mesh(mesh.devices.reshape(4, 2, 8, 2, 2), AXES)
    placed = (P(ROW, COL), P(None, ROW), P(ROW), P(ROW))
    return jax.shard_map(
        local, mesh=split, in_specs=placed, out_specs=(P(None, ROW + COL), P(), P()), check_vma=False
    )
```

```python
import jax
import jax.numpy as jnp
from jax import lax
from jax.experimental import pallas as pl
from jax.experimental.pallas import tpu as pltpu
from jax.sharding import Mesh
from jax.sharding import PartitionSpec as P

N = 32768
S = 32
BODIES = 64
STEPS = 3
ROWS = 512
COLS = 8192
Q = 128
H = 16
AXES = ("y", "xh", "z", "xl", "co")
ROW = ("y", "xh", "z")
COL = ("xl", "co")
MESH = pl.DeviceIdType.MESH
F32 = jnp.float32
BF16 = jnp.bfloat16
OP_CHUNKS = 4
NEAR = (0, 1, 7, 2, 6, 3, 5, 4)


def mm(a, b):
    return lax.dot_general(
        a, b, (((1,), (0,)), ((), ())), precision=lax.Precision.HIGHEST, preferred_element_type=F32
    )


def mm_t(a, b):
    return lax.dot_general(
        a, b, (((1,), (1,)), ((), ())), precision=lax.Precision.HIGHEST, preferred_element_type=F32
    )


def dot_low(a, b):
    return lax.dot_general(a, b, (((1,), (1,)), ((), ())), preferred_element_type=F32)


def factor(gram):
    row_id = lax.broadcasted_iota(jnp.int32, (S, Q), 0)
    lane_id = lax.broadcasted_iota(jnp.int32, (S, Q), 1)
    eye = (lane_id == row_id + S).astype(F32)
    work = jnp.concatenate([gram, jnp.zeros((S, Q - S), F32)], axis=1) + eye
    for k in range(S - 1):
        col = jnp.broadcast_to(work[:, k : k + 1], (S, Q))
        share = jnp.where(row_id > k, col * work[k : k + 1, :], 0.0)
        work = work - share * (1.0 / col[k : k + 1, :])
    pivots = jnp.sum(jnp.where(lane_id == row_id, work, 0.0), axis=1, keepdims=True)
    r = lax.rsqrt(pivots)
    work = work * (r * (1.5 - 0.5 * pivots * r * r))
    upper = jnp.where(lane_id >= row_id, work, 0.0)[:, :S]
    return upper, work[:, S : 2 * S]


def kernel(
    op_hbm,
    rhs_ref,
    bodies_ref,
    weights_ref,
    basis_ref,
    hess_ref,
    start_ref,
    op,
    ext,
    stack,
    wide,
    low,
    mid,
    part,
    parts_in,
    side_out,
    sides_in,
    acc,
    side_acc,
    table_out,
    table_in,
    pay0,
    zc_buf,
    xy_buf,
    total,
    op_sem,
    g_send,
    g0_recv,
    g1_recv,
    gm_recv,
    r_send,
    r_recv,
    s_send,
    s_recv,
    t_sem,
    a_send,
    a_recv,
):
    y, xh, z, xl, co = (lax.axis_index(a) for a in AXES)
    c = xl * 2 + co
    x = xh * 2 + xl
    mine = pl.ds(pl.multiple_of(((xh * 8 + z) * 4 + c) * Q, Q), Q)
    straight = xl == y // 2
    own1 = co == y % 2
    own0 = jnp.logical_and(jnp.logical_and(straight, own1), z % 2 == 0)

    loads = []
    width = COLS // OP_CHUNKS
    for i in range(OP_CHUNKS):
        window = pl.ds(i * width, width)
        loads.append(pltpu.make_async_copy(op_hbm.at[:, window], op.at[:, window], op_sem.at[i]))
        loads[-1].start()

    def plane_to(i):
        return ((y + i % 4) % 4, (xh + (i // 4) % 2) % 2, (z + i // 8) % 8, y // 2, y % 2)

    def plane_from(i):
        return (c, i // 32, (i // 4) % 8, (i // 2) % 2, i % 2)

    def a0_to(i):
        return ((y + 2 * (z % 2)) % 4, (xh + i % 2) % 2, (z + i // 2) % 8, y // 2, y % 2)

    def a0_from(i):
        return (c, i // 16, ((i // 4) % 4) * 2 + ((y + 4 - c) % 4) // 2, (i // 2) % 2, i % 2)

    def a1_to(i):
        return ((y + i % 4) % 4, xh, (z + i // 4) % 8, xl, y % 2)

    def a1_from(i):
        return (co + 2 * (i // 16), xh, (i // 2) % 8, xl, i % 2)

    def zc_peer(i):
        return (y, xh, (z + i // 2) % 8, xl, (co + i) % 2)

    def xy_peer(i):
        t = (x + i) % 4
        return ((y + i // 4) % 4, t // 2, z, t % 2, co)

    def col_peer(i):
        t = (c + i) % 4
        return (y, xh, z, t // 2, t % 2)

    other_core = (y, xh, z, xl, 1 - co)

    barrier = pltpu.get_barrier_semaphore()

    def greet(count, peer, first):
        def body(i, carry):
            pl.semaphore_signal(barrier, inc=1, device_id=peer(i), device_id_type=MESH)
            return carry

        lax.fori_loop(first, count, body, 0)
        return count - first

    root = (y + 4 - c) % 2 == 0

    @pl.when(root)
    def _():
        greet(32, a0_from, 0)

    greeted = 16 + greet(32, a1_from, 0)
    greeted += greet(64, plane_from, 0)
    greeted += greet(16, zc_peer, 1)
    greeted += greet(16, xy_peer, 1)
    greeted += greet(4, col_peer, 1)

    quarter = pl.ds(pl.multiple_of(c * Q, Q), Q)
    weight = weights_ref[:, quarter]
    body = bodies_ref[:, quarter]
    ids = lax.broadcasted_iota(jnp.int32, (BODIES, Q), 0)
    stack[pl.ds(0, BODIES), :] = jnp.where(ids == body, weight, 0.0)
    stack[pl.ds(BODIES, 4 * S), :] = jnp.zeros((4 * S, Q), F32)
    wide[...] = jnp.zeros_like(wide)
    hess_ref[...] = jnp.zeros_like(hess_ref)
    newest = rhs_ref[:, quarter]
    table_out[pl.ds(0, 1), :] = weight
    table_out[pl.ds(1, 1), :] = body.astype(F32)

    pl.semaphore_wait(barrier, greeted)

    pending = []

    def remote(src, dst, send, recv, device):
        return pltpu.make_async_remote_copy(
            src_ref=src, dst_ref=dst, send_sem=send, recv_sem=recv, device_id=device, device_id_type=MESH
        )

    def await_bytes(ref, sem):
        pltpu.make_async_copy(ref, ref, sem).wait()

    def halves(pay):
        h = pay.shape[0] // 2
        return h, pl.ds(pl.multiple_of(co * h, h), h), pl.ds(pl.multiple_of((1 - co) * h, h), h)

    def sum_start(j, pay):
        h, own, theirs = halves(pay)
        here = z * 2 + co
        zc_buf[j, here, pl.ds(0, h), :] = pay[own, :]
        dst = zc_buf.at[j, here, pl.ds(0, h), :]
        for i in (8, 9, 7, 6, 10, 11, 5, 4, 12, 13, 3, 2, 14, 15, 1):
            src = pay.at[theirs if i % 2 else own, :]
            remote(src, dst, a_send.at[j, 0], a_recv.at[j, 0], zc_peer(i)).start()
        pending.append((zc_buf.at[j, pl.ds(0, 15), pl.ds(0, h), :], a_send.at[j, 0]))

    def summed(buf, j, h, count):
        terms = [buf[j, i, :h, :] for i in range(count)]
        while len(terms) > 1:
            terms = [terms[i] + terms[i + 1] for i in range(0, len(terms), 2)]
        return terms[0]

    def sum_middle(j, pay):
        h, _, _ = halves(pay)
        await_bytes(zc_buf.at[j, pl.ds(0, 15), pl.ds(0, h), :], a_recv.at[j, 0])
        here = y * 4 + x
        xy_buf[j, here, pl.ds(0, h), :] = summed(zc_buf, j, h, 16)
        slot = xy_buf.at[j, here, pl.ds(0, h), :]
        for i in (10, 9, 11, 14, 6, 8, 2, 13, 15, 5, 7, 1, 3, 4, 12):
            remote(slot, slot, a_send.at[j, 1], a_recv.at[j, 1], xy_peer(i)).start()
        pending.append((xy_buf.at[j, pl.ds(0, 15), pl.ds(0, h), :], a_send.at[j, 1]))

    def sum_finish(j, pay):
        h, own, theirs = halves(pay)
        await_bytes(xy_buf.at[j, pl.ds(0, 15), pl.ds(0, h), :], a_recv.at[j, 1])
        total[j, own, :] = summed(xy_buf, j, h, 16)
        out = total.at[j, own, :]
        remote(out, out, a_send.at[j, 2], a_recv.at[j, 2], other_core).start()
        pending.append((out, a_send.at[j, 2]))
        await_bytes(total.at[j, theirs, :], a_recv.at[j, 2])

    def top(j):
        return pl.ds(2 * BODIES + S * j, H)

    def low_rows(j):
        return pl.ds(2 * BODIES + S * j + H, H)

    def all_rows(j):
        return pl.ds(2 * BODIES + S * j, S)

    def lanes0(xh_s, z_s):
        return pl.ds(pl.multiple_of((xh_s * 8 + z_s) * 4 * Q, 4 * Q), 4 * Q)

    def lanes1(x_s, z_s):
        return pl.ds(pl.multiple_of((((x_s // 2) * 8 + z_s) * 2 + x_s % 2) * 2 * Q, 2 * Q), 2 * Q)

    def root_for(z_s):
        return (y + 4 - c) % 4 == 2 * (z_s % 2)

    def loop(first, end, do):
        def body(i, carry):
            do(i)
            return carry

        lax.fori_loop(first, end, body, 0)

    def either(test, yes, no):
        pl.when(test)(yes)
        pl.when(jnp.logical_not(test))(no)

    def gather_start(j):
        src1, src0 = low.at[j, pl.ds(H, H), :], low.at[j, pl.ds(0, H), :]
        at1 = ext.at[low_rows(j), mine]
        at_mid = mid.at[j, z, :, pl.ds(pl.multiple_of(co * Q, Q), Q)]
        at0 = ext.at[top(j), mine]
        sem1, sem_mid, sem0 = g1_recv.at[j, x * 8 + z], gm_recv.at[j, z], g0_recv.at[j, xh * 8 + z]

        def spread1(dst, sem):
            loop(4, 32, lambda i: remote(src1, dst, g_send.at[j, 1], sem, a1_to(i)).start())
            loop(1, 4, lambda i: remote(src1, dst, g_send.at[j, 1], sem, a1_to(i)).start())
            either(
                own1,
                lambda: pltpu.make_async_copy(src1, dst, sem).start(),
                lambda: remote(src1, dst, g_send.at[j, 1], sem, a1_to(0)).start(),
            )

        either(straight, lambda: spread1(at1, sem1), lambda: spread1(at_mid, sem_mid))
        loop(1, 16, lambda i: remote(src0, at0, g_send.at[j, 0], sem0, a0_to(i)).start())
        either(
            own0,
            lambda: pltpu.make_async_copy(src0, at0, sem0).start(),
            lambda: remote(src0, at0, g_send.at[j, 0], sem0, a0_to(0)).start(),
        )

    def relay(j, d):
        z_s = (z + d) % 8
        here = ext.at[low_rows(j), lanes1(x, z_s)]
        sem1 = g1_recv.at[j, x * 8 + z_s]
        await_bytes(here, sem1)
        remote(here, here, g_send.at[j, 2], sem1, (y, 1 - xh, z, xl, co)).start()
        held = mid.at[j, z_s]
        await_bytes(held, gm_recv.at[j, z_s])
        for t in range(2):
            remote(held, here, g_send.at[j, 2], sem1, (y, t, z, 1 - xl, co)).start()

        @pl.when(root_for(z_s))
        def _():
            for xh_s in range(2):
                block = ext.at[top(j), lanes0(xh_s, z_s)]
                sem0 = g0_recv.at[j, xh_s * 8 + z_s]
                await_bytes(block, sem0)
                for i in (2, 1, 3):
                    remote(block, block, g_send.at[j, 3], sem0, ((y + i) % 4, xh, z, xl, co)).start()

    def await_z(j, z_s):
        @pl.when(jnp.logical_not(root_for(z_s)))
        def _():
            for xh_s in range(2):
                await_bytes(ext.at[top(j), lanes0(xh_s, z_s)], g0_recv.at[j, xh_s * 8 + z_s])

        for i in range(1, 4):
            x_s = (x + i) % 4
            await_bytes(ext.at[low_rows(j), lanes1(x_s, z_s)], g1_recv.at[j, x_s * 8 + z_s])

    def gather_sent(j):
        either(
            own0,
            lambda: await_bytes(ext.at[top(j), pl.ds(0, 15 * Q)], g_send.at[j, 0]),
            lambda: await_bytes(ext.at[top(j), pl.ds(0, 16 * Q)], g_send.at[j, 0]),
        )
        either(
            own1,
            lambda: await_bytes(ext.at[top(j), pl.ds(0, 31 * Q)], g_send.at[j, 1]),
            lambda: await_bytes(ext.at[top(j), pl.ds(0, 32 * Q)], g_send.at[j, 1]),
        )
        await_bytes(ext.at[top(j), pl.ds(0, 48 * Q)], g_send.at[j, 2])

        @pl.when(root)
        def _():
            await_bytes(ext.at[all_rows(j), pl.ds(0, 48 * Q)], g_send.at[j, 3])

    here = xh * 32 + z * 4 + c
    tables = pl.ds(0, 2)

    def table_start():
        src, dst = table_out.at[tables, :], table_in.at[here, tables, :]
        loop(1, 64, lambda i: remote(src, dst, t_sem.at[0], t_sem.at[1], plane_to(i)).start())
        either(
            jnp.logical_and(straight, own1),
            lambda: pltpu.make_async_copy(src, dst, t_sem.at[1]).start(),
            lambda: remote(src, dst, t_sem.at[0], t_sem.at[1], plane_to(0)).start(),
        )

    def table_finish():
        await_bytes(table_in.at[:, tables, :], t_sem.at[1])

        def build(i):
            plane = jnp.where(ids.astype(F32) == table_in[i, 1:2, :], table_in[i, 0:1, :], 0.0)
            window = pl.ds(pl.multiple_of(i * Q, Q), Q)
            high = plane.astype(BF16)
            ext[pl.ds(0, BODIES), window] = high
            ext[pl.ds(BODIES, BODIES), window] = (plane - high.astype(F32)).astype(BF16)

        loop(0, 64, build)

    def padded(value):
        return jnp.concatenate([value, jnp.zeros((S, Q - value.shape[1]), F32)], axis=1)

    lane = lax.broadcasted_iota(jnp.int32, (S, Q), 1)
    sub = lax.broadcasted_iota(jnp.int32, (S, Q), 0)
    pred = None

    def write_hess(j, coef, upper):
        full = padded(coef + pred).T
        hess_ref[pl.ds(0, S * j), pl.ds(S * (j - 1), S)] = full[: S * j, :]
        hess_ref[pl.ds(S * j, S), pl.ds(S * (j - 1), S)] = upper

    for j in range(STEPS):
        low[j] = newest.astype(BF16)
        gather_start(j)
        if j == 0:
            table_start()
        elif j == 1:
            start_ref[...] = upper.T
        else:
            write_hess(j - 1, coef, upper)
        if j > 0:
            pred = next_pred
        for d in NEAR:
            relay(j, d)
        if j == 0:
            table_finish()
            for load in loads:
                load.wait()
        for n, d in enumerate(NEAR):
            z_s = (z + d) % 8
            await_z(j, z_s)
            pair = (lanes0(0, z_s), lanes0(1, z_s))
            block = jnp.concatenate([ext[all_rows(j), w] for w in pair], axis=1)
            rows = pl.ds(0, 2 * BODIES + S * (j + 1))
            side_term = dot_low(block, jnp.concatenate([ext[rows, w] for w in pair], axis=1))
            term = dot_low(block, jnp.concatenate([op[:, w] for w in pair], axis=1))
            width = 2 * BODIES + S * (j + 1)
            if n > 0:
                term = term + acc[...]
                side_term = side_term + side_acc[:, :width]
            if n < 7:
                acc[...] = term
                side_acc[:, :width] = side_term
        side = side_term[:, BODIES:]
        side = jnp.concatenate([side_term[:, :BODIES] + side[:, :BODIES], side[:, BODIES:]], axis=1)
        side_rows = S + 8 * (j // 2)
        side_out[j, pl.ds(0, S), :] = padded(side) if j < 1 else side[:, :Q]
        if j == 2:
            side_out[j, pl.ds(S, 8), :] = jnp.concatenate([side[8 * i : 8 * i + 8, Q:] for i in range(4)], axis=1)
        out = side_out.at[j, pl.ds(0, side_rows), :]
        for i in (2, 3, 1):
            remote(out, sides_in.at[j, c, pl.ds(0, side_rows), :], s_send.at[j], s_recv.at[j], col_peer(i)).start()
        three = sides_in.at[j, pl.ds(0, 3), pl.ds(0, side_rows), :]
        pending.append((three, s_send.at[j]))
        for i in range(4):
            part[j, i] = term[:, i * Q : (i + 1) * Q]
        for i in range(1, 4):
            remote(part.at[j, (c + i) % 4], parts_in.at[j, c], r_send.at[j], r_recv.at[j], col_peer(i)).start()
        pending.append((part.at[j, pl.ds(0, 3)], r_send.at[j]))
        parts_in[j, c] = part[j, c]
        sides_in[j, c, pl.ds(0, side_rows), :] = side_out[j, :side_rows, :]
        await_bytes(three, s_recv.at[j])
        sums = [sides_in[j, i, :side_rows, :] for i in range(4)]
        sums = (sums[0] + sums[1]) + (sums[2] + sums[3])
        sums, extra = sums[:S], sums[S:]
        mean = sums[:, :BODIES] * (BODIES / N)
        raw = sums[:, BODIES:] * (1.0 / N)
        if j == 2:
            extra = jnp.concatenate([extra[:, S * i : S * i + S] for i in range(4)], axis=0)
            raw = jnp.concatenate([raw, extra * (1.0 / N)], axis=1)
        gram = raw[:, S * j : S * (j + 1)]
        coef = None
        if j > 0:
            coef = mm_t(padded(raw[:, : S * j]), wide[pl.ds(0, S * j), pl.ds(3 * Q, Q)])
            gram = gram - mm_t(coef, coef)
        upper, inverse = factor(gram)
        completion = mm(mean, stack[pl.ds(0, BODIES), :])
        await_bytes(parts_in.at[j, pl.ds(0, 3)], r_recv.at[j])
        coupled = (parts_in[j, 0] + parts_in[j, 1]) + (parts_in[j, 2] + parts_in[j, 3])
        image = 0.5 * newest + completion + coupled
        full = jnp.concatenate([newest, image, padded(mean), jnp.where(lane == sub + S * j, 1.0, 0.0)], axis=1)
        if j > 0:
            full = full - mm(coef, wide[pl.ds(0, S * j), :])
        full = mm(inverse, full)
        wide[pl.ds(S * j, S), :] = full
        upto = pl.ds(0, S * (j + 1))
        next_pred = mm_t(full[:, 2 * Q : 3 * Q], wide[upto, pl.ds(2 * Q, Q)]) * (1.0 / BODIES)
        next_pred = next_pred + jnp.where(lane == sub + S * j, 0.5, 0.0)[:, : S * (j + 1)]
        newest = full[:, Q : 2 * Q] - mm(next_pred, wide[upto, pl.ds(0, Q)])

    for j in range(STEPS):
        basis_ref[pl.ds(S * j, S), :] = wide[pl.ds(S * j, S), pl.ds(0, Q)]
        stack[pl.ds(BODIES + S * j, S), :] = wide[pl.ds(S * j, S), pl.ds(0, Q)]
    stack[pl.ds(BODIES + S * STEPS, S), :] = newest
    pay0[...] = mm_t(newest, stack[pl.ds(BODIES, 4 * S), :])
    sum_start(0, pay0)
    write_hess(2, coef, upper)
    pred = next_pred
    for i in range(STEPS):
        gather_sent(i)
    either(
        jnp.logical_and(straight, own1),
        lambda: await_bytes(table_in.at[pl.ds(0, 63), tables, :], t_sem.at[0]),
        lambda: await_bytes(table_in.at[:, tables, :], t_sem.at[0]),
    )
    sum_middle(0, pay0)
    sum_finish(0, pay0)
    sums = total[0] * (1.0 / N)
    coef, gram = sums[:, : 3 * S], sums[:, 3 * S :]
    gram = gram - mm_t(coef, coef)
    residual = newest - mm(coef, stack[pl.ds(BODIES, 3 * S), :])
    upper, inverse = factor(gram)
    basis_ref[pl.ds(3 * S, S), :] = mm(inverse, residual)
    write_hess(3, coef, upper)

    for ref, sem in pending:
        await_bytes(ref, sem)


def local(operator, rhs, bodies, weights):
    vmem = pl.BlockSpec(memory_space=pltpu.VMEM)
    dma = pltpu.SemaphoreType.DMA
    return pl.pallas_call(
        kernel,
        name="arnoldi",
        out_shape=(
            jax.ShapeDtypeStruct((4 * S, Q), F32),
            jax.ShapeDtypeStruct((4 * S, 3 * S), F32),
            jax.ShapeDtypeStruct((S, S), F32),
        ),
        in_specs=[pl.BlockSpec(memory_space=pl.ANY), vmem, vmem, vmem],
        out_specs=(vmem, vmem, vmem),
        scratch_shapes=[
            pltpu.VMEM((ROWS, COLS), BF16),
            pltpu.VMEM((2 * BODIES + 3 * S, COLS), BF16),
            pltpu.VMEM((BODIES + 4 * S, Q), F32),
            pltpu.VMEM((3 * S, 4 * Q), F32),
            pltpu.VMEM((3, S, Q), BF16),
            pltpu.VMEM((3, 8, H, 2 * Q), BF16),
            pltpu.VMEM((3, 4, S, Q), F32),
            pltpu.VMEM((3, 4, S, Q), F32),
            pltpu.VMEM((3, S + 8, Q), F32),
            pltpu.VMEM((3, 4, S + 8, Q), F32),
            pltpu.VMEM((S, ROWS), F32),
            pltpu.VMEM((S, 2 * Q), F32),
            pltpu.VMEM((8, Q), F32),
            pltpu.VMEM((64, 8, Q), F32),
            pltpu.VMEM((S, Q), F32),
            pltpu.VMEM((1, 16, H, Q), F32),
            pltpu.VMEM((1, 16, H, Q), F32),
            pltpu.VMEM((1, S, Q), F32),
            dma((OP_CHUNKS,)),
            dma((3, 4)),
            dma((3, 16)),
            dma((3, 32)),
            dma((3, 8)),
            dma((3,)),
            dma((3,)),
            dma((3,)),
            dma((3,)),
            dma((2,)),
            dma((1, 3)),
            dma((1, 3)),
        ],
        compiler_params=pltpu.CompilerParams(
            collective_id=0, has_side_effects=True, vmem_limit_bytes=40 * 2**20
        ),
    )(operator, rhs, bodies.reshape(1, ROWS), weights.reshape(1, ROWS))


def solution(mesh):
    split = Mesh(mesh.devices.reshape(4, 2, 8, 2, 2), AXES)
    placed = (P(ROW, COL), P(None, ROW), P(ROW), P(ROW))
    return jax.shard_map(
        local, mesh=split, in_specs=placed, out_specs=(P(None, ROW + COL), P(), P()), check_vma=False
    )
```

```python
import jax
import jax.numpy as jnp
from jax import lax
from jax.experimental import pallas as pl
from jax.experimental.pallas import tpu as pltpu
from jax.sharding import Mesh
from jax.sharding import PartitionSpec as P

N = 32768
S = 32
BODIES = 64
STEPS = 3
ROWS = 512
COLS = 8192
Q = 128
H = 16
AXES = ("y", "xh", "z", "xl", "co")
ROW = ("y", "xh", "z")
COL = ("xl", "co")
MESH = pl.DeviceIdType.MESH
F32 = jnp.float32
BF16 = jnp.bfloat16
OP_CHUNKS = 4
NEAR = (0, 1, 7, 2, 6, 3, 5, 4)
FAR = (4, 5, 3, 6, 2, 7, 1, 0)


def mm(a, b):
    return lax.dot_general(
        a, b, (((1,), (0,)), ((), ())), precision=lax.Precision.HIGHEST, preferred_element_type=F32
    )


def mm_t(a, b):
    return lax.dot_general(
        a, b, (((1,), (1,)), ((), ())), precision=lax.Precision.HIGHEST, preferred_element_type=F32
    )


def dot_low(a, b):
    return lax.dot_general(a, b, (((1,), (1,)), ((), ())), preferred_element_type=F32)


def factor(gram):
    row_id = lax.broadcasted_iota(jnp.int32, (S, Q), 0)
    lane_id = lax.broadcasted_iota(jnp.int32, (S, Q), 1)
    eye = (lane_id == row_id + S).astype(F32)
    work = jnp.concatenate([gram, jnp.zeros((S, Q - S), F32)], axis=1) + eye
    for k in range(S - 1):
        col = jnp.broadcast_to(work[:, k : k + 1], (S, Q))
        share = jnp.where(row_id > k, col * work[k : k + 1, :], 0.0)
        work = work - share * (1.0 / col[k : k + 1, :])
    pivots = jnp.sum(jnp.where(lane_id == row_id, work, 0.0), axis=1, keepdims=True)
    r = lax.rsqrt(pivots)
    work = work * (r * (1.5 - 0.5 * pivots * r * r))
    upper = jnp.where(lane_id >= row_id, work, 0.0)[:, :S]
    return upper, work[:, S : 2 * S]


def kernel(
    op_hbm,
    rhs_ref,
    bodies_ref,
    weights_ref,
    basis_ref,
    hess_ref,
    start_ref,
    op,
    ext,
    stack,
    wide,
    low,
    mid,
    part,
    parts_in,
    side_out,
    sides_in,
    acc,
    side_acc,
    table_out,
    table_in,
    pay0,
    zc_buf,
    xy_buf,
    total,
    op_sem,
    g_send,
    g0_recv,
    g1_recv,
    gm_recv,
    r_send,
    r_recv,
    s_send,
    s_recv,
    t_sem,
    a_send,
    a_recv,
):
    y, xh, z, xl, co = (lax.axis_index(a) for a in AXES)
    c = xl * 2 + co
    x = xh * 2 + xl
    mine = pl.ds(pl.multiple_of(((xh * 8 + z) * 4 + c) * Q, Q), Q)
    straight = xl == y // 2
    own1 = co == y % 2
    own0 = jnp.logical_and(jnp.logical_and(straight, own1), z % 2 == 0)

    loads = []
    width = COLS // OP_CHUNKS
    for i in range(OP_CHUNKS):
        window = pl.ds(i * width, width)
        loads.append(pltpu.make_async_copy(op_hbm.at[:, window], op.at[:, window], op_sem.at[i]))
        loads[-1].start()

    def plane_to(i):
        return ((y + i % 4) % 4, (xh + (i // 4) % 2) % 2, (z + i // 8) % 8, y // 2, y % 2)

    def plane_from(i):
        return (c, i // 32, (i // 4) % 8, (i // 2) % 2, i % 2)

    def a0_to(i):
        return ((y + 2 * (z % 2)) % 4, (xh + i % 2) % 2, (z + i // 2) % 8, y // 2, y % 2)

    def a0_from(i):
        return (c, i // 16, ((i // 4) % 4) * 2 + ((y + 4 - c) % 4) // 2, (i // 2) % 2, i % 2)

    def a1_to(i):
        return ((y + i % 4) % 4, xh, (z + i // 4) % 8, xl, y % 2)

    def a1_from(i):
        return (co + 2 * (i // 16), xh, (i // 2) % 8, xl, i % 2)

    def zc_peer(i):
        return (y, xh, (z + i // 2) % 8, xl, (co + i) % 2)

    def xy_peer(i):
        t = (x + i) % 4
        return ((y + i // 4) % 4, t // 2, z, t % 2, co)

    def col_peer(i):
        t = (c + i) % 4
        return (y, xh, z, t // 2, t % 2)

    other_core = (y, xh, z, xl, 1 - co)

    barrier = pltpu.get_barrier_semaphore()

    def greet(count, peer, first):
        for i in range(first, count):
            pl.semaphore_signal(barrier, inc=1, device_id=peer(i), device_id_type=MESH)
        return count - first

    root = (y + 4 - c) % 2 == 0

    @pl.when(root)
    def _():
        greet(32, a0_from, 0)

    greeted = 16 + greet(32, a1_from, 0)
    greeted += greet(64, plane_from, 0)
    greeted += greet(16, zc_peer, 1)
    greeted += greet(16, xy_peer, 1)
    greeted += greet(4, col_peer, 1)

    quarter = pl.ds(pl.multiple_of(c * Q, Q), Q)
    weight = weights_ref[:, quarter]
    body = bodies_ref[:, quarter]
    ids = lax.broadcasted_iota(jnp.int32, (BODIES, Q), 0)
    stack[pl.ds(0, BODIES), :] = jnp.where(ids == body, weight, 0.0)
    stack[pl.ds(BODIES, 4 * S), :] = jnp.zeros((4 * S, Q), F32)
    wide[...] = jnp.zeros_like(wide)
    hess_ref[...] = jnp.zeros_like(hess_ref)
    newest = rhs_ref[:, quarter]
    table_out[pl.ds(0, 1), :] = weight
    table_out[pl.ds(1, 1), :] = body.astype(F32)

    pl.semaphore_wait(barrier, greeted)

    pending = []

    def remote(src, dst, send, recv, device):
        return pltpu.make_async_remote_copy(
            src_ref=src, dst_ref=dst, send_sem=send, recv_sem=recv, device_id=device, device_id_type=MESH
        )

    def await_bytes(ref, sem):
        pltpu.make_async_copy(ref, ref, sem).wait()

    def halves(pay):
        h = pay.shape[0] // 2
        return h, pl.ds(pl.multiple_of(co * h, h), h), pl.ds(pl.multiple_of((1 - co) * h, h), h)

    def sum_start(j, pay):
        h, own, theirs = halves(pay)
        here = z * 2 + co
        zc_buf[j, here, pl.ds(0, h), :] = pay[own, :]
        dst = zc_buf.at[j, here, pl.ds(0, h), :]
        for i in (8, 9, 7, 6, 10, 11, 5, 4, 12, 13, 3, 2, 14, 15, 1):
            src = pay.at[theirs if i % 2 else own, :]
            remote(src, dst, a_send.at[j, 0], a_recv.at[j, 0], zc_peer(i)).start()
        pending.append((zc_buf.at[j, pl.ds(0, 15), pl.ds(0, h), :], a_send.at[j, 0]))

    def summed(buf, j, h, count):
        terms = [buf[j, i, :h, :] for i in range(count)]
        while len(terms) > 1:
            terms = [terms[i] + terms[i + 1] for i in range(0, len(terms), 2)]
        return terms[0]

    def sum_middle(j, pay):
        h, _, _ = halves(pay)
        await_bytes(zc_buf.at[j, pl.ds(0, 15), pl.ds(0, h), :], a_recv.at[j, 0])
        here = y * 4 + x
        xy_buf[j, here, pl.ds(0, h), :] = summed(zc_buf, j, h, 16)
        slot = xy_buf.at[j, here, pl.ds(0, h), :]
        for i in (10, 9, 11, 14, 6, 8, 2, 13, 15, 5, 7, 1, 3, 4, 12):
            remote(slot, slot, a_send.at[j, 1], a_recv.at[j, 1], xy_peer(i)).start()
        pending.append((xy_buf.at[j, pl.ds(0, 15), pl.ds(0, h), :], a_send.at[j, 1]))

    def sum_finish(j, pay):
        h, own, theirs = halves(pay)
        await_bytes(xy_buf.at[j, pl.ds(0, 15), pl.ds(0, h), :], a_recv.at[j, 1])
        total[j, own, :] = summed(xy_buf, j, h, 16)
        out = total.at[j, own, :]
        remote(out, out, a_send.at[j, 2], a_recv.at[j, 2], other_core).start()
        pending.append((out, a_send.at[j, 2]))
        await_bytes(total.at[j, theirs, :], a_recv.at[j, 2])

    def top(j):
        return pl.ds(2 * BODIES + S * j, H)

    def low_rows(j):
        return pl.ds(2 * BODIES + S * j + H, H)

    def all_rows(j):
        return pl.ds(2 * BODIES + S * j, S)

    def lanes0(xh_s, z_s):
        return pl.ds(pl.multiple_of((xh_s * 8 + z_s) * 4 * Q, 4 * Q), 4 * Q)

    def lanes1(x_s, z_s):
        return pl.ds(pl.multiple_of((((x_s // 2) * 8 + z_s) * 2 + x_s % 2) * 2 * Q, 2 * Q), 2 * Q)

    def root_for(z_s):
        return (y + 4 - c) % 4 == 2 * (z_s % 2)

    def loop(first, end, do):
        def body(i, carry):
            do(i)
            return carry

        lax.fori_loop(first, end, body, 0)

    def either(test, yes, no):
        pl.when(test)(yes)
        pl.when(jnp.logical_not(test))(no)

    def gather_start(j):
        src1, src0 = low.at[j, pl.ds(H, H), :], low.at[j, pl.ds(0, H), :]
        at1 = ext.at[low_rows(j), mine]
        at_mid = mid.at[j, z, :, pl.ds(pl.multiple_of(co * Q, Q), Q)]
        at0 = ext.at[top(j), mine]
        sem1, sem_mid, sem0 = g1_recv.at[j, x * 8 + z], gm_recv.at[j, z], g0_recv.at[j, xh * 8 + z]

        def spread(dst, sem):
            for d in FAR:
                for i in (2, 1, 3, 0):
                    if d or i:
                        remote(src1, dst, g_send.at[j, 1], sem, a1_to(4 * d + i)).start()
                for i in (1, 0):
                    if d or i:
                        remote(src0, at0, g_send.at[j, 0], sem0, a0_to(2 * d + i)).start()
            either(
                own1,
                lambda: pltpu.make_async_copy(src1, dst, sem).start(),
                lambda: remote(src1, dst, g_send.at[j, 1], sem, a1_to(0)).start(),
            )

        either(straight, lambda: spread(at1, sem1), lambda: spread(at_mid, sem_mid))
        either(
            own0,
            lambda: pltpu.make_async_copy(src0, at0, sem0).start(),
            lambda: remote(src0, at0, g_send.at[j, 0], sem0, a0_to(0)).start(),
        )

    def relay(j, d):
        z_s = (z + d) % 8
        here = ext.at[low_rows(j), lanes1(x, z_s)]
        sem1 = g1_recv.at[j, x * 8 + z_s]
        await_bytes(here, sem1)
        remote(here, here, g_send.at[j, 2], sem1, (y, 1 - xh, z, xl, co)).start()
        held = mid.at[j, z_s]
        await_bytes(held, gm_recv.at[j, z_s])
        for t in range(2):
            remote(held, here, g_send.at[j, 2], sem1, (y, t, z, 1 - xl, co)).start()

        @pl.when(root_for(z_s))
        def _():
            for xh_s in range(2):
                block = ext.at[top(j), lanes0(xh_s, z_s)]
                sem0 = g0_recv.at[j, xh_s * 8 + z_s]
                await_bytes(block, sem0)
                for i in (2, 1, 3):
                    remote(block, block, g_send.at[j, 3], sem0, ((y + i) % 4, xh, z, xl, co)).start()

    def await_z(j, z_s):
        @pl.when(jnp.logical_not(root_for(z_s)))
        def _():
            for xh_s in range(2):
                await_bytes(ext.at[top(j), lanes0(xh_s, z_s)], g0_recv.at[j, xh_s * 8 + z_s])

        for i in range(1, 4):
            x_s = (x + i) % 4
            await_bytes(ext.at[low_rows(j), lanes1(x_s, z_s)], g1_recv.at[j, x_s * 8 + z_s])

    def gather_sent(j):
        either(
            own0,
            lambda: await_bytes(ext.at[top(j), pl.ds(0, 15 * Q)], g_send.at[j, 0]),
            lambda: await_bytes(ext.at[top(j), pl.ds(0, 16 * Q)], g_send.at[j, 0]),
        )
        either(
            own1,
            lambda: await_bytes(ext.at[top(j), pl.ds(0, 31 * Q)], g_send.at[j, 1]),
            lambda: await_bytes(ext.at[top(j), pl.ds(0, 32 * Q)], g_send.at[j, 1]),
        )
        await_bytes(ext.at[top(j), pl.ds(0, 48 * Q)], g_send.at[j, 2])

        @pl.when(root)
        def _():
            await_bytes(ext.at[all_rows(j), pl.ds(0, 48 * Q)], g_send.at[j, 3])

    here = xh * 32 + z * 4 + c
    tables = pl.ds(0, 2)

    def table_start():
        src, dst = table_out.at[tables, :], table_in.at[here, tables, :]
        for d in FAR:
            for i in range(8 * d, 8 * d + 8):
                if i:
                    remote(src, dst, t_sem.at[0], t_sem.at[1], plane_to(i)).start()
        either(
            jnp.logical_and(straight, own1),
            lambda: pltpu.make_async_copy(src, dst, t_sem.at[1]).start(),
            lambda: remote(src, dst, t_sem.at[0], t_sem.at[1], plane_to(0)).start(),
        )

    def table_finish():
        await_bytes(table_in.at[:, tables, :], t_sem.at[1])

        def build(k):
            for t in range(4):
                i = 4 * k + t
                plane = jnp.where(ids_f == table_in[i, 1:2, :], table_in[i, 0:1, :], 0.0)
                window = pl.ds(pl.multiple_of(i * Q, Q), Q)
                high = plane.astype(BF16)
                ext[pl.ds(0, BODIES), window] = high
                ext[pl.ds(BODIES, BODIES), window] = (plane - high.astype(F32)).astype(BF16)

        ids_f = ids.astype(F32)
        loop(0, 16, build)

    def padded(value):
        return jnp.concatenate([value, jnp.zeros((S, Q - value.shape[1]), F32)], axis=1)

    lane = lax.broadcasted_iota(jnp.int32, (S, Q), 1)
    sub = lax.broadcasted_iota(jnp.int32, (S, Q), 0)
    pred = None

    def write_hess(j, coef, upper):
        full = padded(coef + pred).T
        hess_ref[pl.ds(0, S * j), pl.ds(S * (j - 1), S)] = full[: S * j, :]
        hess_ref[pl.ds(S * j, S), pl.ds(S * (j - 1), S)] = upper

    for j in range(STEPS):
        low[j] = newest.astype(BF16)
        gather_start(j)
        if j == 0:
            table_start()
        elif j == 1:
            start_ref[...] = upper.T
        else:
            write_hess(j - 1, coef, upper)
        if j > 0:
            pred = next_pred
        for d in NEAR:
            relay(j, d)
        if j == 0:
            table_finish()
            for load in loads:
                load.wait()
        for n, d in enumerate(NEAR):
            z_s = (z + d) % 8
            await_z(j, z_s)
            pair = (lanes0(0, z_s), lanes0(1, z_s))
            block = jnp.concatenate([ext[all_rows(j), w] for w in pair], axis=1)
            rows = pl.ds(0, 2 * BODIES + S * (j + 1))
            side_term = dot_low(block, jnp.concatenate([ext[rows, w] for w in pair], axis=1))
            term = dot_low(block, jnp.concatenate([op[:, w] for w in pair], axis=1))
            width = 2 * BODIES + S * (j + 1)
            if n > 0:
                term = term + acc[...]
                side_term = side_term + side_acc[:, :width]
            if n < 7:
                acc[...] = term
                side_acc[:, :width] = side_term
        side = side_term[:, BODIES:]
        side = jnp.concatenate([side_term[:, :BODIES] + side[:, :BODIES], side[:, BODIES:]], axis=1)
        side_rows = S + 8 * (j // 2)
        side_out[j, pl.ds(0, S), :] = padded(side) if j < 1 else side[:, :Q]
        if j == 2:
            side_out[j, pl.ds(S, 8), :] = jnp.concatenate([side[8 * i : 8 * i + 8, Q:] for i in range(4)], axis=1)
        out = side_out.at[j, pl.ds(0, side_rows), :]
        for i in (2, 3, 1):
            remote(out, sides_in.at[j, c, pl.ds(0, side_rows), :], s_send.at[j], s_recv.at[j], col_peer(i)).start()
        three = sides_in.at[j, pl.ds(0, 3), pl.ds(0, side_rows), :]
        pending.append((three, s_send.at[j]))
        for i in range(4):
            part[j, i] = term[:, i * Q : (i + 1) * Q]
        for i in range(1, 4):
            remote(part.at[j, (c + i) % 4], parts_in.at[j, c], r_send.at[j], r_recv.at[j], col_peer(i)).start()
        pending.append((part.at[j, pl.ds(0, 3)], r_send.at[j]))
        parts_in[j, c] = part[j, c]
        sides_in[j, c, pl.ds(0, side_rows), :] = side_out[j, :side_rows, :]
        await_bytes(three, s_recv.at[j])
        sums = [sides_in[j, i, :side_rows, :] for i in range(4)]
        sums = (sums[0] + sums[1]) + (sums[2] + sums[3])
        sums, extra = sums[:S], sums[S:]
        mean = sums[:, :BODIES] * (BODIES / N)
        raw = sums[:, BODIES:] * (1.0 / N)
        if j == 2:
            extra = jnp.concatenate([extra[:, S * i : S * i + S] for i in range(4)], axis=0)
            raw = jnp.concatenate([raw, extra * (1.0 / N)], axis=1)
        gram = raw[:, S * j : S * (j + 1)]
        coef = None
        if j > 0:
            coef = mm_t(padded(raw[:, : S * j]), wide[pl.ds(0, S * j), pl.ds(3 * Q, Q)])
            gram = gram - mm_t(coef, coef)
        upper, inverse = factor(gram)
        completion = mm(mean, stack[pl.ds(0, BODIES), :])
        await_bytes(parts_in.at[j, pl.ds(0, 3)], r_recv.at[j])
        coupled = (parts_in[j, 0] + parts_in[j, 1]) + (parts_in[j, 2] + parts_in[j, 3])
        image = 0.5 * newest + completion + coupled
        full = jnp.concatenate([newest, image, padded(mean), jnp.where(lane == sub + S * j, 1.0, 0.0)], axis=1)
        if j > 0:
            full = full - mm(coef, wide[pl.ds(0, S * j), :])
        full = mm(inverse, full)
        wide[pl.ds(S * j, S), :] = full
        upto = pl.ds(0, S * (j + 1))
        next_pred = mm_t(full[:, 2 * Q : 3 * Q], wide[upto, pl.ds(2 * Q, Q)]) * (1.0 / BODIES)
        next_pred = next_pred + jnp.where(lane == sub + S * j, 0.5, 0.0)[:, : S * (j + 1)]
        newest = full[:, Q : 2 * Q] - mm(next_pred, wide[upto, pl.ds(0, Q)])

    for j in range(STEPS):
        basis_ref[pl.ds(S * j, S), :] = wide[pl.ds(S * j, S), pl.ds(0, Q)]
        stack[pl.ds(BODIES + S * j, S), :] = wide[pl.ds(S * j, S), pl.ds(0, Q)]
    stack[pl.ds(BODIES + S * STEPS, S), :] = newest
    pay0[...] = mm_t(newest, stack[pl.ds(BODIES, 4 * S), :])
    sum_start(0, pay0)
    write_hess(2, coef, upper)
    pred = next_pred
    for i in range(STEPS):
        gather_sent(i)
    either(
        jnp.logical_and(straight, own1),
        lambda: await_bytes(table_in.at[pl.ds(0, 63), tables, :], t_sem.at[0]),
        lambda: await_bytes(table_in.at[:, tables, :], t_sem.at[0]),
    )
    sum_middle(0, pay0)
    sum_finish(0, pay0)
    sums = total[0] * (1.0 / N)
    coef, gram = sums[:, : 3 * S], sums[:, 3 * S :]
    gram = gram - mm_t(coef, coef)
    residual = newest - mm(coef, stack[pl.ds(BODIES, 3 * S), :])
    upper, inverse = factor(gram)
    basis_ref[pl.ds(3 * S, S), :] = mm(inverse, residual)
    write_hess(3, coef, upper)

    for ref, sem in pending:
        await_bytes(ref, sem)


def local(operator, rhs, bodies, weights):
    vmem = pl.BlockSpec(memory_space=pltpu.VMEM)
    dma = pltpu.SemaphoreType.DMA
    return pl.pallas_call(
        kernel,
        name="arnoldi",
        out_shape=(
            jax.ShapeDtypeStruct((4 * S, Q), F32),
            jax.ShapeDtypeStruct((4 * S, 3 * S), F32),
            jax.ShapeDtypeStruct((S, S), F32),
        ),
        in_specs=[pl.BlockSpec(memory_space=pl.ANY), vmem, vmem, vmem],
        out_specs=(vmem, vmem, vmem),
        scratch_shapes=[
            pltpu.VMEM((ROWS, COLS), BF16),
            pltpu.VMEM((2 * BODIES + 3 * S, COLS), BF16),
            pltpu.VMEM((BODIES + 4 * S, Q), F32),
            pltpu.VMEM((3 * S, 4 * Q), F32),
            pltpu.VMEM((3, S, Q), BF16),
            pltpu.VMEM((3, 8, H, 2 * Q), BF16),
            pltpu.VMEM((3, 4, S, Q), F32),
            pltpu.VMEM((3, 4, S, Q), F32),
            pltpu.VMEM((3, S + 8, Q), F32),
            pltpu.VMEM((3, 4, S + 8, Q), F32),
            pltpu.VMEM((S, ROWS), F32),
            pltpu.VMEM((S, 2 * Q), F32),
            pltpu.VMEM((8, Q), F32),
            pltpu.VMEM((64, 8, Q), F32),
            pltpu.VMEM((S, Q), F32),
            pltpu.VMEM((1, 16, H, Q), F32),
            pltpu.VMEM((1, 16, H, Q), F32),
            pltpu.VMEM((1, S, Q), F32),
            dma((OP_CHUNKS,)),
            dma((3, 4)),
            dma((3, 16)),
            dma((3, 32)),
            dma((3, 8)),
            dma((3,)),
            dma((3,)),
            dma((3,)),
            dma((3,)),
            dma((2,)),
            dma((1, 3)),
            dma((1, 3)),
        ],
        compiler_params=pltpu.CompilerParams(
            collective_id=0, has_side_effects=True, vmem_limit_bytes=40 * 2**20
        ),
    )(operator, rhs, bodies.reshape(1, ROWS), weights.reshape(1, ROWS))


def solution(mesh):
    split = Mesh(mesh.devices.reshape(4, 2, 8, 2, 2), AXES)
    placed = (P(ROW, COL), P(None, ROW), P(ROW), P(ROW))
    return jax.shard_map(
        local, mesh=split, in_specs=placed, out_specs=(P(None, ROW + COL), P(), P()), check_vma=False
    )
```

```python
import jax
import jax.numpy as jnp
from jax import lax
from jax.experimental import pallas as pl
from jax.experimental.pallas import tpu as pltpu
from jax.sharding import Mesh
from jax.sharding import PartitionSpec as P

N = 32768
S = 32
BODIES = 64
STEPS = 3
ROWS = 512
COLS = 8192
Q = 128
H = 16
AXES = ("y", "xh", "z", "xl", "co")
ROW = ("y", "xh", "z")
COL = ("xl", "co")
MESH = pl.DeviceIdType.MESH
F32 = jnp.float32
BF16 = jnp.bfloat16
OP_CHUNKS = 4
NEAR = (0, 1, 7, 2, 6, 3, 5, 4)
FAR = (4, 5, 3, 6, 2, 7, 1, 0)


def mm(a, b):
    return lax.dot_general(
        a, b, (((1,), (0,)), ((), ())), precision=lax.Precision.HIGHEST, preferred_element_type=F32
    )


def mm_t(a, b):
    return lax.dot_general(
        a, b, (((1,), (1,)), ((), ())), precision=lax.Precision.HIGHEST, preferred_element_type=F32
    )


def dot_low(a, b):
    return lax.dot_general(a, b, (((1,), (1,)), ((), ())), preferred_element_type=F32)


def factor(gram):
    row_id = lax.broadcasted_iota(jnp.int32, (S, Q), 0)
    lane_id = lax.broadcasted_iota(jnp.int32, (S, Q), 1)
    eye = (lane_id == row_id + S).astype(F32)
    work = jnp.concatenate([gram, jnp.zeros((S, Q - S), F32)], axis=1) + eye
    for k in range(0, S, 2):
        a = jnp.broadcast_to(work[:, k : k + 1], (S, Q))
        b = jnp.broadcast_to(work[:, k + 1 : k + 2], (S, Q))
        first, second = work[k : k + 1, :], work[k + 1 : k + 2, :]
        scale = 1.0 / a[k : k + 1, :]
        first = first * scale
        second = second - a[k + 1 : k + 2, :] * first
        b = b - a * (b[k : k + 1, :] * scale)
        rest = work - a * first - b * (second * (1.0 / b[k + 1 : k + 2, :]))
        work = jnp.where(row_id > k + 1, rest, jnp.where(row_id == k + 1, second, work))
    pivots = jnp.sum(jnp.where(lane_id == row_id, work, 0.0), axis=1, keepdims=True)
    r = lax.rsqrt(pivots)
    work = work * (r * (1.5 - 0.5 * pivots * r * r))
    upper = jnp.where(lane_id >= row_id, work, 0.0)[:, :S]
    return upper, work[:, S : 2 * S]


def kernel(
    op_hbm,
    rhs_ref,
    bodies_ref,
    weights_ref,
    basis_ref,
    hess_ref,
    start_ref,
    op,
    ext,
    stack,
    wide,
    low,
    mid,
    part,
    parts_in,
    side_out,
    sides_in,
    acc,
    side_acc,
    table_out,
    table_in,
    pay0,
    zc_buf,
    xy_buf,
    total,
    op_sem,
    g_send,
    g0_recv,
    g1_recv,
    gm_recv,
    r_send,
    r_recv,
    s_send,
    s_recv,
    t_sem,
    a_send,
    a_recv,
):
    y, xh, z, xl, co = (lax.axis_index(a) for a in AXES)
    c = xl * 2 + co
    x = xh * 2 + xl
    mine = pl.ds(pl.multiple_of(((xh * 8 + z) * 4 + c) * Q, Q), Q)
    straight = xl == y // 2
    own1 = co == y % 2
    own0 = jnp.logical_and(jnp.logical_and(straight, own1), z % 2 == 0)

    loads = []
    width = COLS // OP_CHUNKS
    for i in range(OP_CHUNKS):
        window = pl.ds(i * width, width)
        loads.append(pltpu.make_async_copy(op_hbm.at[:, window], op.at[:, window], op_sem.at[i]))
        loads[-1].start()

    def plane_to(i):
        return ((y + i % 4) % 4, (xh + (i // 4) % 2) % 2, (z + i // 8) % 8, y // 2, y % 2)

    def plane_from(i):
        return (c, i // 32, (i // 4) % 8, (i // 2) % 2, i % 2)

    def a0_to(i):
        return ((y + 2 * (z % 2)) % 4, (xh + i % 2) % 2, (z + i // 2) % 8, y // 2, y % 2)

    def a0_from(i):
        return (c, i // 16, ((i // 4) % 4) * 2 + ((y + 4 - c) % 4) // 2, (i // 2) % 2, i % 2)

    def a1_to(i):
        return ((y + i % 4) % 4, xh, (z + i // 4) % 8, xl, y % 2)

    def a1_from(i):
        return (co + 2 * (i // 16), xh, (i // 2) % 8, xl, i % 2)

    def zc_peer(i):
        return (y, xh, (z + i // 2) % 8, xl, (co + i) % 2)

    def xy_peer(i):
        t = (x + i) % 4
        return ((y + i // 4) % 4, t // 2, z, t % 2, co)

    def col_peer(i):
        t = (c + i) % 4
        return (y, xh, z, t // 2, t % 2)

    other_core = (y, xh, z, xl, 1 - co)

    barrier = pltpu.get_barrier_semaphore()

    def greet(count, peer, first):
        for i in range(first, count):
            pl.semaphore_signal(barrier, inc=1, device_id=peer(i), device_id_type=MESH)
        return count - first

    root = (y + 4 - c) % 2 == 0

    @pl.when(root)
    def _():
        greet(32, a0_from, 0)

    greeted = 16 + greet(32, a1_from, 0)
    greeted += greet(64, plane_from, 0)
    greeted += greet(16, zc_peer, 1)
    greeted += greet(16, xy_peer, 1)
    greeted += greet(4, col_peer, 1)

    quarter = pl.ds(pl.multiple_of(c * Q, Q), Q)
    weight = weights_ref[:, quarter]
    body = bodies_ref[:, quarter]
    ids = lax.broadcasted_iota(jnp.int32, (BODIES, Q), 0)
    stack[pl.ds(0, BODIES), :] = jnp.where(ids == body, weight, 0.0)
    stack[pl.ds(BODIES, 4 * S), :] = jnp.zeros((4 * S, Q), F32)
    wide[...] = jnp.zeros_like(wide)
    hess_ref[...] = jnp.zeros_like(hess_ref)
    newest = rhs_ref[:, quarter]
    table_out[pl.ds(0, 1), :] = weight
    table_out[pl.ds(1, 1), :] = body.astype(F32)

    pl.semaphore_wait(barrier, greeted)

    pending = []

    def remote(src, dst, send, recv, device):
        return pltpu.make_async_remote_copy(
            src_ref=src, dst_ref=dst, send_sem=send, recv_sem=recv, device_id=device, device_id_type=MESH
        )

    def await_bytes(ref, sem):
        pltpu.make_async_copy(ref, ref, sem).wait()

    def halves(pay):
        h = pay.shape[0] // 2
        return h, pl.ds(pl.multiple_of(co * h, h), h), pl.ds(pl.multiple_of((1 - co) * h, h), h)

    def sum_start(j, pay):
        h, own, theirs = halves(pay)
        here = z * 2 + co
        zc_buf[j, here, pl.ds(0, h), :] = pay[own, :]
        dst = zc_buf.at[j, here, pl.ds(0, h), :]
        for i in (8, 9, 7, 6, 10, 11, 5, 4, 12, 13, 3, 2, 14, 15, 1):
            src = pay.at[theirs if i % 2 else own, :]
            remote(src, dst, a_send.at[j, 0], a_recv.at[j, 0], zc_peer(i)).start()
        pending.append((zc_buf.at[j, pl.ds(0, 15), pl.ds(0, h), :], a_send.at[j, 0]))

    def summed(buf, j, h, count):
        terms = [buf[j, i, :h, :] for i in range(count)]
        while len(terms) > 1:
            terms = [terms[i] + terms[i + 1] for i in range(0, len(terms), 2)]
        return terms[0]

    def sum_middle(j, pay):
        h, _, _ = halves(pay)
        await_bytes(zc_buf.at[j, pl.ds(0, 15), pl.ds(0, h), :], a_recv.at[j, 0])
        here = y * 4 + x
        xy_buf[j, here, pl.ds(0, h), :] = summed(zc_buf, j, h, 16)
        slot = xy_buf.at[j, here, pl.ds(0, h), :]
        for i in (10, 9, 11, 14, 6, 8, 2, 13, 15, 5, 7, 1, 3, 4, 12):
            remote(slot, slot, a_send.at[j, 1], a_recv.at[j, 1], xy_peer(i)).start()
        pending.append((xy_buf.at[j, pl.ds(0, 15), pl.ds(0, h), :], a_send.at[j, 1]))

    def sum_finish(j, pay):
        h, own, theirs = halves(pay)
        await_bytes(xy_buf.at[j, pl.ds(0, 15), pl.ds(0, h), :], a_recv.at[j, 1])
        total[j, own, :] = summed(xy_buf, j, h, 16)
        out = total.at[j, own, :]
        remote(out, out, a_send.at[j, 2], a_recv.at[j, 2], other_core).start()
        pending.append((out, a_send.at[j, 2]))
        await_bytes(total.at[j, theirs, :], a_recv.at[j, 2])

    def top(j):
        return pl.ds(2 * BODIES + S * j, H)

    def low_rows(j):
        return pl.ds(2 * BODIES + S * j + H, H)

    def all_rows(j):
        return pl.ds(2 * BODIES + S * j, S)

    def lanes0(xh_s, z_s):
        return pl.ds(pl.multiple_of((xh_s * 8 + z_s) * 4 * Q, 4 * Q), 4 * Q)

    def lanes1(x_s, z_s):
        return pl.ds(pl.multiple_of((((x_s // 2) * 8 + z_s) * 2 + x_s % 2) * 2 * Q, 2 * Q), 2 * Q)

    def root_for(z_s):
        return (y + 4 - c) % 4 == 2 * (z_s % 2)

    def loop(first, end, do):
        def body(i, carry):
            do(i)
            return carry

        lax.fori_loop(first, end, body, 0)

    def either(test, yes, no):
        pl.when(test)(yes)
        pl.when(jnp.logical_not(test))(no)

    def gather_start(j):
        src1, src0 = low.at[j, pl.ds(H, H), :], low.at[j, pl.ds(0, H), :]
        at1 = ext.at[low_rows(j), mine]
        at_mid = mid.at[j, z, :, pl.ds(pl.multiple_of(co * Q, Q), Q)]
        at0 = ext.at[top(j), mine]
        sem1, sem_mid, sem0 = g1_recv.at[j, x * 8 + z], gm_recv.at[j, z], g0_recv.at[j, xh * 8 + z]

        def spread(dst, sem):
            for d in FAR:
                for i in (2, 1, 3, 0):
                    if d or i:
                        remote(src1, dst, g_send.at[j, 1], sem, a1_to(4 * d + i)).start()
                for i in (1, 0):
                    if d or i:
                        remote(src0, at0, g_send.at[j, 0], sem0, a0_to(2 * d + i)).start()
            either(
                own1,
                lambda: pltpu.make_async_copy(src1, dst, sem).start(),
                lambda: remote(src1, dst, g_send.at[j, 1], sem, a1_to(0)).start(),
            )

        either(straight, lambda: spread(at1, sem1), lambda: spread(at_mid, sem_mid))
        either(
            own0,
            lambda: pltpu.make_async_copy(src0, at0, sem0).start(),
            lambda: remote(src0, at0, g_send.at[j, 0], sem0, a0_to(0)).start(),
        )

    def relay(j, d):
        z_s = (z + d) % 8
        here = ext.at[low_rows(j), lanes1(x, z_s)]
        sem1 = g1_recv.at[j, x * 8 + z_s]
        await_bytes(here, sem1)
        remote(here, here, g_send.at[j, 2], sem1, (y, 1 - xh, z, xl, co)).start()
        held = mid.at[j, z_s]
        await_bytes(held, gm_recv.at[j, z_s])
        for t in range(2):
            remote(held, here, g_send.at[j, 2], sem1, (y, t, z, 1 - xl, co)).start()

        @pl.when(root_for(z_s))
        def _():
            for xh_s in range(2):
                block = ext.at[top(j), lanes0(xh_s, z_s)]
                sem0 = g0_recv.at[j, xh_s * 8 + z_s]
                await_bytes(block, sem0)
                for i in (2, 1, 3):
                    remote(block, block, g_send.at[j, 3], sem0, ((y + i) % 4, xh, z, xl, co)).start()

    def await_z(j, z_s):
        @pl.when(jnp.logical_not(root_for(z_s)))
        def _():
            for xh_s in range(2):
                await_bytes(ext.at[top(j), lanes0(xh_s, z_s)], g0_recv.at[j, xh_s * 8 + z_s])

        for i in range(1, 4):
            x_s = (x + i) % 4
            await_bytes(ext.at[low_rows(j), lanes1(x_s, z_s)], g1_recv.at[j, x_s * 8 + z_s])

    def gather_sent(j):
        either(
            own0,
            lambda: await_bytes(ext.at[top(j), pl.ds(0, 15 * Q)], g_send.at[j, 0]),
            lambda: await_bytes(ext.at[top(j), pl.ds(0, 16 * Q)], g_send.at[j, 0]),
        )
        either(
            own1,
            lambda: await_bytes(ext.at[top(j), pl.ds(0, 31 * Q)], g_send.at[j, 1]),
            lambda: await_bytes(ext.at[top(j), pl.ds(0, 32 * Q)], g_send.at[j, 1]),
        )
        await_bytes(ext.at[top(j), pl.ds(0, 48 * Q)], g_send.at[j, 2])

        @pl.when(root)
        def _():
            await_bytes(ext.at[all_rows(j), pl.ds(0, 48 * Q)], g_send.at[j, 3])

    here = xh * 32 + z * 4 + c
    tables = pl.ds(0, 2)

    def table_start():
        src, dst = table_out.at[tables, :], table_in.at[here, tables, :]
        for d in FAR:
            for i in range(8 * d, 8 * d + 8):
                if i:
                    remote(src, dst, t_sem.at[0], t_sem.at[1], plane_to(i)).start()
        either(
            jnp.logical_and(straight, own1),
            lambda: pltpu.make_async_copy(src, dst, t_sem.at[1]).start(),
            lambda: remote(src, dst, t_sem.at[0], t_sem.at[1], plane_to(0)).start(),
        )

    def table_finish():
        await_bytes(table_in.at[:, tables, :], t_sem.at[1])

        def build(k):
            for t in range(4):
                i = 4 * k + t
                plane = jnp.where(ids_f == table_in[i, 1:2, :], table_in[i, 0:1, :], 0.0)
                window = pl.ds(pl.multiple_of(i * Q, Q), Q)
                high = plane.astype(BF16)
                ext[pl.ds(0, BODIES), window] = high
                ext[pl.ds(BODIES, BODIES), window] = (plane - high.astype(F32)).astype(BF16)

        ids_f = ids.astype(F32)
        loop(0, 16, build)

    def padded(value):
        return jnp.concatenate([value, jnp.zeros((S, Q - value.shape[1]), F32)], axis=1)

    lane = lax.broadcasted_iota(jnp.int32, (S, Q), 1)
    sub = lax.broadcasted_iota(jnp.int32, (S, Q), 0)
    pred = None

    def write_hess(j, coef, upper):
        full = padded(coef + pred).T
        hess_ref[pl.ds(0, S * j), pl.ds(S * (j - 1), S)] = full[: S * j, :]
        hess_ref[pl.ds(S * j, S), pl.ds(S * (j - 1), S)] = upper

    for j in range(STEPS):
        low[j] = newest.astype(BF16)
        gather_start(j)
        if j == 0:
            table_start()
        elif j == 1:
            start_ref[...] = upper.T
        else:
            write_hess(j - 1, coef, upper)
        if j > 0:
            pred = next_pred
        for d in NEAR:
            relay(j, d)
        if j == 0:
            table_finish()
            for load in loads:
                load.wait()
        for n, d in enumerate(NEAR):
            z_s = (z + d) % 8
            await_z(j, z_s)
            pair = (lanes0(0, z_s), lanes0(1, z_s))
            block = jnp.concatenate([ext[all_rows(j), w] for w in pair], axis=1)
            rows = pl.ds(0, 2 * BODIES + S * (j + 1))
            side_term = dot_low(block, jnp.concatenate([ext[rows, w] for w in pair], axis=1))
            term = dot_low(block, jnp.concatenate([op[:, w] for w in pair], axis=1))
            width = 2 * BODIES + S * (j + 1)
            if n > 0:
                term = term + acc[...]
                side_term = side_term + side_acc[:, :width]
            if n < 7:
                acc[...] = term
                side_acc[:, :width] = side_term
        side = side_term[:, BODIES:]
        side = jnp.concatenate([side_term[:, :BODIES] + side[:, :BODIES], side[:, BODIES:]], axis=1)
        side_rows = S + 8 * (j // 2)
        side_out[j, pl.ds(0, S), :] = padded(side) if j < 1 else side[:, :Q]
        if j == 2:
            side_out[j, pl.ds(S, 8), :] = jnp.concatenate([side[8 * i : 8 * i + 8, Q:] for i in range(4)], axis=1)
        out = side_out.at[j, pl.ds(0, side_rows), :]
        for i in (2, 3, 1):
            remote(out, sides_in.at[j, c, pl.ds(0, side_rows), :], s_send.at[j], s_recv.at[j], col_peer(i)).start()
        three = sides_in.at[j, pl.ds(0, 3), pl.ds(0, side_rows), :]
        pending.append((three, s_send.at[j]))
        for i in range(4):
            part[j, i] = term[:, i * Q : (i + 1) * Q]
        for i in range(1, 4):
            remote(part.at[j, (c + i) % 4], parts_in.at[j, c], r_send.at[j], r_recv.at[j], col_peer(i)).start()
        pending.append((part.at[j, pl.ds(0, 3)], r_send.at[j]))
        parts_in[j, c] = part[j, c]
        sides_in[j, c, pl.ds(0, side_rows), :] = side_out[j, :side_rows, :]
        await_bytes(three, s_recv.at[j])
        sums = [sides_in[j, i, :side_rows, :] for i in range(4)]
        sums = (sums[0] + sums[1]) + (sums[2] + sums[3])
        sums, extra = sums[:S], sums[S:]
        mean = sums[:, :BODIES] * (BODIES / N)
        raw = sums[:, BODIES:] * (1.0 / N)
        if j == 2:
            extra = jnp.concatenate([extra[:, S * i : S * i + S] for i in range(4)], axis=0)
            raw = jnp.concatenate([raw, extra * (1.0 / N)], axis=1)
        gram = raw[:, S * j : S * (j + 1)]
        coef = None
        if j > 0:
            coef = mm_t(padded(raw[:, : S * j]), wide[pl.ds(0, S * j), pl.ds(3 * Q, Q)])
            gram = gram - mm_t(coef, coef)
        upper, inverse = factor(gram)
        completion = mm(mean, stack[pl.ds(0, BODIES), :])
        await_bytes(parts_in.at[j, pl.ds(0, 3)], r_recv.at[j])
        coupled = (parts_in[j, 0] + parts_in[j, 1]) + (parts_in[j, 2] + parts_in[j, 3])
        image = 0.5 * newest + completion + coupled
        full = jnp.concatenate([newest, image, padded(mean), jnp.where(lane == sub + S * j, 1.0, 0.0)], axis=1)
        if j > 0:
            full = full - mm(coef, wide[pl.ds(0, S * j), :])
        full = mm(inverse, full)
        wide[pl.ds(S * j, S), :] = full
        upto = pl.ds(0, S * (j + 1))
        next_pred = mm_t(full[:, 2 * Q : 3 * Q], wide[upto, pl.ds(2 * Q, Q)]) * (1.0 / BODIES)
        next_pred = next_pred + jnp.where(lane == sub + S * j, 0.5, 0.0)[:, : S * (j + 1)]
        newest = full[:, Q : 2 * Q] - mm(next_pred, wide[upto, pl.ds(0, Q)])

    for j in range(STEPS):
        basis_ref[pl.ds(S * j, S), :] = wide[pl.ds(S * j, S), pl.ds(0, Q)]
        stack[pl.ds(BODIES + S * j, S), :] = wide[pl.ds(S * j, S), pl.ds(0, Q)]
    stack[pl.ds(BODIES + S * STEPS, S), :] = newest
    pay0[...] = mm_t(newest, stack[pl.ds(BODIES, 4 * S), :])
    sum_start(0, pay0)
    write_hess(2, coef, upper)
    pred = next_pred
    for i in range(STEPS):
        gather_sent(i)
    either(
        jnp.logical_and(straight, own1),
        lambda: await_bytes(table_in.at[pl.ds(0, 63), tables, :], t_sem.at[0]),
        lambda: await_bytes(table_in.at[:, tables, :], t_sem.at[0]),
    )
    sum_middle(0, pay0)
    sum_finish(0, pay0)
    sums = total[0] * (1.0 / N)
    coef, gram = sums[:, : 3 * S], sums[:, 3 * S :]
    gram = gram - mm_t(coef, coef)
    residual = newest - mm(coef, stack[pl.ds(BODIES, 3 * S), :])
    upper, inverse = factor(gram)
    basis_ref[pl.ds(3 * S, S), :] = mm(inverse, residual)
    write_hess(3, coef, upper)

    for ref, sem in pending:
        await_bytes(ref, sem)


def local(operator, rhs, bodies, weights):
    vmem = pl.BlockSpec(memory_space=pltpu.VMEM)
    dma = pltpu.SemaphoreType.DMA
    return pl.pallas_call(
        kernel,
        name="arnoldi",
        out_shape=(
            jax.ShapeDtypeStruct((4 * S, Q), F32),
            jax.ShapeDtypeStruct((4 * S, 3 * S), F32),
            jax.ShapeDtypeStruct((S, S), F32),
        ),
        in_specs=[pl.BlockSpec(memory_space=pl.ANY), vmem, vmem, vmem],
        out_specs=(vmem, vmem, vmem),
        scratch_shapes=[
            pltpu.VMEM((ROWS, COLS), BF16),
            pltpu.VMEM((2 * BODIES + 3 * S, COLS), BF16),
            pltpu.VMEM((BODIES + 4 * S, Q), F32),
            pltpu.VMEM((3 * S, 4 * Q), F32),
            pltpu.VMEM((3, S, Q), BF16),
            pltpu.VMEM((3, 8, H, 2 * Q), BF16),
            pltpu.VMEM((3, 4, S, Q), F32),
            pltpu.VMEM((3, 4, S, Q), F32),
            pltpu.VMEM((3, S + 8, Q), F32),
            pltpu.VMEM((3, 4, S + 8, Q), F32),
            pltpu.VMEM((S, ROWS), F32),
            pltpu.VMEM((S, 2 * Q), F32),
            pltpu.VMEM((8, Q), F32),
            pltpu.VMEM((64, 8, Q), F32),
            pltpu.VMEM((S, Q), F32),
            pltpu.VMEM((1, 16, H, Q), F32),
            pltpu.VMEM((1, 16, H, Q), F32),
            pltpu.VMEM((1, S, Q), F32),
            dma((OP_CHUNKS,)),
            dma((3, 4)),
            dma((3, 16)),
            dma((3, 32)),
            dma((3, 8)),
            dma((3,)),
            dma((3,)),
            dma((3,)),
            dma((3,)),
            dma((2,)),
            dma((1, 3)),
            dma((1, 3)),
        ],
        compiler_params=pltpu.CompilerParams(
            collective_id=0, has_side_effects=True, vmem_limit_bytes=40 * 2**20
        ),
    )(operator, rhs, bodies.reshape(1, ROWS), weights.reshape(1, ROWS))


def solution(mesh):
    split = Mesh(mesh.devices.reshape(4, 2, 8, 2, 2), AXES)
    placed = (P(ROW, COL), P(None, ROW), P(ROW), P(ROW))
    return jax.shard_map(
        local, mesh=split, in_specs=placed, out_specs=(P(None, ROW + COL), P(), P()), check_vma=False
    )
```
